512 devices in a mesh: seq: 64 (over x, z), head: 8 (over y, core).
Axes of the slice: x: 4, y: 4, z: 16, core: 2. Of those that a mesh axis runs over, the one named last changes fastest.
Arguments:
- query: bfloat16 [8192, 4096], P('seq', 'head'), may hold values from -20 to 20
- keys: bfloat16 [8192, 4096], P('seq', 'head'), may hold values from -6 to 6
- values: bfloat16 [8192, 4096], P('seq', 'head'), may hold values from -20 to 20
- grad_normed: bfloat16 [8192, 4096], P('seq', 'head'), may hold values from -18 to 18
- norm_gain: float32 [4096], P('head'), may hold values from 0.25 to 1.75
- doc_ids: int32 [8192], P('seq'), may hold values from 0 to 15, never falling along the last dimension, each value on 1 to 1024 neighbouring positions
- home: int32 [8192], P('seq'), may hold values from 0 to 8191, as said below
Outputs:
- input_grads: bfloat16 [8192, 3, 4096], P('seq', None, 'head')
The draws below stay inside these ranges and needn't reach their ends.
Inputs may be any that keep to these rules, and one draw needn't show every extreme that they name: home is a permutation of 0 to 8191; the owner index along seq of token t is home[t] // 128. Of the 128 tokens on one index of seq, at most 4 have one owner index, and that many is reached for some pairs; every index of seq sends the same multiset of counts to the owners, in a drawn order of owners.
All inputs are finite; a program needn't handle non-finite values.
Results may differ from the reference program's by a relative error of at most 0.0058.
Values may be sent and summed in bfloat16 or wider, within the bound.
No kernel may reach another device: no remote copies, remote signals or barrier semaphores. Data moves between devices by JAX's collectives and lax.ppermute only.
A program may use at most 128 MiB of HBM per device.

```python
import math
import jax
import jax.numpy as jnp
import numpy as np
from jax import lax

TOK_DEV = 128
HEADS = 32
HS = 128
TOKENS = 8192
DOCS = 16
DOC_MOST = 1024
N_SEQ = 64


def draw_query(key, part):
    base_key, row_key = jax.random.split(jax.random.fold_in(key, 11))
    shape = (TOKENS, HEADS * HS)
    base = jnp.clip(jax.random.normal(base_key, shape, jnp.float32), -4.0, 4.0)
    row_scale = jnp.exp(jax.random.uniform(row_key, (TOKENS, 1), jnp.float32, math.log(0.5), math.log(5.0)))
    return (base * row_scale).astype(jnp.bfloat16)


def draw_values(key, part):
    base_key, column_key = jax.random.split(jax.random.fold_in(key, 17))
    shape = (TOKENS, HEADS * HS)
    head_of = (jnp.arange(HEADS * HS) // HS).astype(jnp.float32)
    rise = head_of / max(HEADS - 1, 1)
    noise = jnp.exp(jax.random.uniform(column_key, (HEADS * HS,), jnp.float32, 0.0, math.log(2.0)))
    base = jnp.clip(jax.random.normal(base_key, shape, jnp.float32), -4.0, 4.0)
    column_scale = 0.25 * jnp.exp(math.log(10.0) * rise) * noise
    return (base * column_scale[None, :]).astype(jnp.bfloat16)


def draw_home(key, part):
    count = N_SEQ
    per_dev = TOK_DEV
    bound = 2 * per_dev // count
    heavy = max(1, count // 8)
    remain = per_dev - heavy * bound
    share = remain // (count - heavy)
    extra = remain - share * (count - heavy)
    pattern = np.array([bound] * heavy + [share + 1] * extra + [share] * (count - heavy - extra), dtype=np.int32)
    offset_key, label_key, owner_key, source_key = jax.random.split(jax.random.fold_in(key, 23), 4)
    weights = jnp.asarray(pattern)[jax.random.permutation(offset_key, count)]
    labels = jax.random.permutation(label_key, count)
    unlabel = jnp.argsort(labels)
    offsets = jnp.arange(count, dtype=jnp.int32)
    owner_of = unlabel[(labels[:, None] + offsets[None, :]) % count]
    counts = jnp.zeros((count, count), jnp.int32).at[offsets[:, None], owner_of].set(jnp.broadcast_to(weights[None, :], (count, count)))
    base = jnp.cumsum(counts, axis=0) - counts
    which = jnp.repeat(offsets, weights, total_repeat_length=per_dev)
    start = jnp.cumsum(weights) - weights
    within = jnp.arange(per_dev, dtype=jnp.int32) - start[which]
    owner = owner_of[:, which]
    slot = base[offsets[:, None], owner] + within[None, :]
    owner_orders = jax.vmap(lambda one: jax.random.permutation(one, per_dev))(jax.random.split(owner_key, count))
    row_in_owner = owner_orders[owner, slot]
    homes = owner * per_dev + row_in_owner
    source_orders = jax.vmap(lambda one: jax.random.permutation(one, per_dev))(jax.random.split(source_key, count))
    homes = jnp.take_along_axis(homes, source_orders, axis=1)
    return homes.reshape(-1).astype(jnp.int32)


def levels(rng, shape, cuts, low, top_value):
    gain, own = 1.0, jax.random.fold_in(rng, 6)
    for axis_at, blocks in cuts:
        heights = jnp.exp(jax.random.uniform(jax.random.fold_in(own, axis_at), (blocks,), jnp.float32, low / len(cuts), top_value / len(cuts)))
        gain = gain * jnp.repeat(heights, shape[axis_at] // blocks).reshape([-1 if axis == axis_at else 1 for axis in range(len(shape))])
    return gain


def profile(amount, total, most, skew):
    loads = [(1 << 20) // math.isqrt(grade ** skew) + 1 for grade in range(2, amount + 1)]
    surplus, holding = total - most - (amount - 1), [1] * (amount - 1)
    while surplus > 0:
        free = [i for i in range(amount - 1) if holding[i] < most]
        pool, remaining = sum([loads[i] for i in free]), surplus
        for i in free:
            addition = min(most - holding[i], max(1, remaining * loads[i] // pool), surplus)
            holding[i] = holding[i] + addition
            surplus = surplus - addition
    return np.array([most] + holding)


def ragged(key, amount, total, most, slope):
    if amount == 2:
        one = jax.random.randint(key, (), max(1, total - most), min(most, total - 1) + 1)
        return jnp.stack([one, total - one])
    sizes = jnp.asarray(profile(amount, total, most, slope), jnp.int32)
    twos = (amount - 1) // 2
    giver, sink = sizes[1:1 + 2 * twos:2], sizes[2:2 + 2 * twos:2]
    margin = jnp.minimum(giver - 1, most - sink)
    shifted = jax.random.randint(jax.random.fold_in(key, 1), (twos,), 0, 1 << 20) % (margin + 1)
    sizes = sizes.at[1:1 + 2 * twos:2].set(giver - shifted).at[2:2 + 2 * twos:2].set(sink + shifted)
    return sizes[jax.random.permutation(jax.random.fold_in(key, 2), amount)]


def centred(rng, dims, spread, most, pieces=(), kind=jnp.bfloat16):
    values = jax.random.normal(rng, dims, jnp.float32) * spread
    if len(pieces) > 0:
        values = levels(rng, dims, pieces, -0.22, 0.18) * values
    return jnp.clip(values, min=-most, max=most).astype(kind)


def setup_inputs(seed: int = 0) -> dict:
    splits = jax.random.split(jax.random.key(seed), 8)
    return {
        "query": draw_query(jax.random.fold_in(splits[7], 71), 0),
        "keys": centred(splits[1], (TOKENS, HEADS * HS), 1.0, 6.0, ((0, 64), (1, 8))),
        "values": draw_values(jax.random.fold_in(splits[7], 71), 0),
        "grad_normed": centred(splits[3], (TOKENS, HEADS * HS), 3.0, 18.0, ((0, 64), (1, 8))),
        "norm_gain": jnp.clip(1.0 + 0.15 * jax.random.normal(splits[4], (HEADS * HS,), jnp.float32), 0.25, 1.75),
        "doc_ids": jnp.searchsorted(jnp.cumsum(ragged(splits[5], DOCS, TOKENS, DOC_MOST, 1)), jnp.arange(TOKENS), side="right").astype(jnp.int32),
        "home": draw_home(jax.random.fold_in(splits[7], 71), 0),
    }


EPSILON = 1e-05
LOW_SENTINEL = -1.0
HIGH_SENTINEL = 1000000000.0

def masked_scores(left, right, doc_block):
    places = jnp.arange(doc_block.shape[0])
    visible = (doc_block[:, None] == doc_block[None, :]) & (places[:, None] >= places[None, :])
    raw = jnp.einsum('thd,shd->hts', left.astype(jnp.float32), right.astype(jnp.float32))
    return jnp.where(visible[None], raw, 0.0).astype(jnp.bfloat16)

def outer_sum(left, right, keep):
    kept = jnp.where(keep[:, None, None], left, jnp.zeros_like(left))
    return jnp.einsum('tha,thb->hab', kept.astype(jnp.float32), right.astype(jnp.float32))

def join_high(earlier, later):
    top = jnp.maximum(earlier[0], later[0])
    state = jnp.where(earlier[0] == top, earlier[1], 0.0) + jnp.where(later[0] == top, later[1], 0.0)
    return (top, state)

def join_low(earlier, later):
    bottom = jnp.minimum(earlier[0], later[0])
    state = jnp.where(earlier[0] == bottom, earlier[1], 0.0) + jnp.where(later[0] == bottom, later[1], 0.0)
    return (bottom, state)

def mixed(left, right, form):
    return jnp.einsum(form, left.astype(jnp.float32), right.astype(jnp.float32))

def reference(query, keys, values, grad_normed, norm_gain, doc_ids, home):
    full_width = HEADS * HS

    def split(array):
        return array.reshape(N_SEQ, TOK_DEV, HEADS, HS)
    query_b = split(query)
    keys_b = split(keys)
    values_b = split(values)
    normed_b = grad_normed.reshape(N_SEQ, TOK_DEV, full_width)
    doc_b = doc_ids.reshape(N_SEQ, TOK_DEV)
    first_keys = doc_b[:, 0].astype(jnp.float32)
    last_keys = doc_b[:, -1].astype(jnp.float32)

    def forward_own(items):
        keys_one, values_one, doc_one = items
        return outer_sum(keys_one, values_one, doc_one == doc_one[-1])
    own_forward = lax.map(forward_own, (keys_b, values_b, doc_b))
    zero_state = jnp.zeros((HEADS, HS, HS), jnp.float32)

    def forward_step(carry, item):
        return (join_high(carry, item), carry)
    _, (fwd_key, fwd_state) = lax.scan(forward_step, (jnp.array(LOW_SENTINEL, jnp.float32), zero_state), (last_keys, own_forward))

    def section_one(items):
        query_one, keys_one, values_one, normed_one, doc_one, carry_key, carry_state = items
        first_rows = (doc_one == doc_one[0])[:, None, None]
        carry = jnp.where(carry_key == doc_one[0].astype(jnp.float32), carry_state, 0.0).astype(jnp.bfloat16)
        attn = masked_scores(query_one, keys_one, doc_one)
        output = mixed(attn, values_one, 'hts,shd->thd') + jnp.where(first_rows, mixed(query_one, carry, 'tha,hab->thb'), 0.0)
        flat = output.reshape(TOK_DEV, full_width)
        scaled = norm_gain[None, :] * normed_one.astype(jnp.float32)
        squares = lax.optimization_barrier(jnp.sum(flat * flat, axis=1))
        inner = lax.optimization_barrier(jnp.sum(scaled * flat, axis=1))
        inv_rms = lax.rsqrt(squares / full_width + EPSILON)
        grad_out = (inv_rms[:, None] * scaled - flat * (inv_rms * inv_rms * inv_rms * inner / full_width)[:, None]).astype(jnp.bfloat16)
        grad_h = grad_out.reshape(TOK_DEV, HEADS, HS)
        back = masked_scores(grad_h, values_one, doc_one)
        grad_query = mixed(back, keys_one, 'hts,shd->thd') + jnp.where(first_rows, mixed(grad_h, carry, 'thb,hab->tha'), 0.0)
        own_reverse = outer_sum(query_one, grad_h, doc_one == doc_one[0])
        return (grad_h, grad_query.astype(jnp.bfloat16).reshape(TOK_DEV, full_width), own_reverse)
    grad_out_b, grad_query_b, own_reverse = lax.map(section_one, (query_b, keys_b, values_b, normed_b, doc_b, fwd_key, fwd_state))

    def reverse_step(carry, item):
        return (join_low(carry, item), carry)
    _, (rev_key, rev_state) = lax.scan(reverse_step, (jnp.array(HIGH_SENTINEL, jnp.float32), zero_state), (first_keys, own_reverse), reverse=True)

    def section_two(items):
        query_one, keys_one, values_one, grad_h, doc_one, carry_key, carry_state = items
        last_rows = (doc_one == doc_one[-1])[:, None, None]
        carry = jnp.where(carry_key == doc_one[-1].astype(jnp.float32), carry_state, 0.0).astype(jnp.bfloat16)
        attn = masked_scores(query_one, keys_one, doc_one)
        back = masked_scores(grad_h, values_one, doc_one)
        grad_keys = mixed(back, query_one, 'hts,thd->shd') + jnp.where(last_rows, mixed(values_one, carry, 'thb,hab->tha'), 0.0)
        grad_values = mixed(attn, grad_h, 'hts,thd->shd') + jnp.where(last_rows, mixed(keys_one, carry, 'tha,hab->thb'), 0.0)
        return (grad_keys.astype(jnp.bfloat16).reshape(TOK_DEV, full_width), grad_values.astype(jnp.bfloat16).reshape(TOK_DEV, full_width))
    grad_keys_b, grad_values_b = lax.map(section_two, (query_b, keys_b, values_b, grad_out_b, doc_b, rev_key, rev_state))
    rows = jnp.stack([grad_query_b.reshape(TOKENS, full_width), grad_keys_b.reshape(TOKENS, full_width), grad_values_b.reshape(TOKENS, full_width)], axis=1)
    return jnp.zeros_like(rows).at[home].set(rows)
```

```python
import jax
import jax.numpy as jnp
from jax import lax
from jax.sharding import PartitionSpec as P

HEADS = 32
HS = 128
EPSILON = 1e-05
SUB = 4
EXTRA = 16


def mixed(left, right, form):
    return jnp.einsum(form, left, right, preferred_element_type=jnp.float32)


def heads_first(array):
    tok_rows, width = array.shape
    return array.reshape(tok_rows, width // HS, HS).transpose(1, 0, 2)


def local(query, keys, values, grad_normed, norm_gain, doc_ids, home):
    tok_rows, width = query.shape
    full_width = HEADS * HS
    seq_count = lax.axis_size("seq")
    head_count = lax.axis_size("head")
    capacity = 2 * tok_rows // seq_count
    groups = [[g * SUB + s for s in range(SUB)] for g in range(seq_count // SUB)]
    wide_groups = [[i * head_count + h for i in one for h in range(head_count)] for one in groups]
    mine = lax.axis_index("seq") % SUB

    owner = home // tok_rows
    target_row = home % tok_rows
    places = jnp.arange(tok_rows)
    same_owner = owner[:, None] == owner[None, :]
    ranks = jnp.sum(jnp.where(same_owner & (places[None, :] < places[:, None]), 1, 0), axis=1)
    local_slot = owner * capacity + ranks
    slot_match = local_slot[None, :] == jnp.arange(seq_count * capacity)[:, None]
    row_index = jnp.max(jnp.where(slot_match, target_row[None, :], -1), axis=1)
    row_index = row_index.reshape(seq_count, capacity)

    def regroup(arrays):
        return lax.all_to_all(
            jnp.concatenate(arrays, axis=1), "seq", 0, 0, tiled=True, axis_index_groups=groups
        )

    small = jnp.stack([doc_ids, owner, ranks]).astype(jnp.bfloat16)
    small = jnp.pad(small, ((0, EXTRA - 3), (0, 0)))
    small = jnp.broadcast_to(small[None], (SUB, EXTRA, tok_rows))
    key_value = regroup([heads_first(keys), heads_first(values), small])
    query_grad = regroup([heads_first(query), heads_first(grad_normed)])
    key = key_value[:, :tok_rows]
    value = key_value[:, tok_rows : 2 * tok_rows]
    small = key_value[:, 2 * tok_rows :]
    doc = small[:, 0].astype(jnp.int32)
    slot = (small[:, 1].astype(jnp.int32) * SUB + jnp.arange(SUB)[:, None]) * capacity
    slot = (slot + small[:, 2].astype(jnp.int32)).reshape(-1)
    quer = query_grad[:, :tok_rows]
    normed = query_grad[:, tok_rows:]

    first, last = doc[:, 0], doc[:, -1]
    first_rows = (doc == first[:, None])[:, :, None]
    last_rows = (doc == last[:, None])[:, :, None]
    zero = jnp.zeros((), jnp.bfloat16)

    def exchange(state, doc_number, sign):
        payload = jnp.concatenate(
            [state.astype(jnp.bfloat16), jnp.full((EXTRA, HS), doc_number, jnp.bfloat16)], axis=0
        )
        pieces = []
        for far in (1, 2):
            step = sign * far * SUB
            pairs = [(i, i + step) for i in range(seq_count) if 0 <= i + step < seq_count]
            pieces.append(lax.ppermute(payload, "seq", pairs))
        return pieces

    def arriving(pieces, doc_number):
        doc_number = doc_number.astype(jnp.bfloat16)
        return sum(
            jnp.where(p[HS, 0] == doc_number, p[:HS].astype(jnp.float32), 0.0) for p in pieces
        )

    sent = mixed(jnp.where((doc == last[-1])[:, :, None], key, zero), value, "bta,btc->ac")
    pieces = exchange(sent, last[-1], 1)
    own = mixed(jnp.where(last_rows, key, zero), value, "bta,btc->bac")
    places = jnp.arange(tok_rows)
    visible = (doc[:, :, None] == doc[:, None, :]) & (places[:, None] >= places[None, :])
    attn = jnp.where(visible, mixed(quer, key, "bta,bsa->bts"), 0.0).astype(jnp.bfloat16)
    state = arriving(pieces, first[0])
    carries = [state]
    for b in range(1, SUB):
        state = own[b - 1] + jnp.where(first[b - 1] == last[b - 1], state, 0.0)
        state = jnp.where(last[b - 1] == first[b], state, 0.0)
        carries.append(state)
    carry = jnp.stack(carries).astype(jnp.bfloat16)
    output = mixed(attn, value, "bts,bsc->btc") + jnp.where(
        first_rows, mixed(quer, carry, "bta,bac->btc"), 0.0
    )
    gain = lax.dynamic_slice(norm_gain, (mine * HS,), (HS,))
    scaled = gain * normed.astype(jnp.float32)
    sums = jnp.concatenate([jnp.sum(output * output, -1), jnp.sum(scaled * output, -1)])
    sums = jnp.broadcast_to(sums[None], (SUB * head_count, 2 * SUB, tok_rows))
    sums = lax.all_to_all(
        sums, ("seq", "head"), 0, 0, tiled=True, axis_index_groups=wide_groups
    ).sum(0)
    squares, inner = sums[:SUB, :, None], sums[SUB:, :, None]
    inv_rms = lax.rsqrt(squares / full_width + EPSILON)
    grad = (
        inv_rms * scaled - output * (inv_rms * inv_rms * inv_rms * inner / full_width)
    ).astype(jnp.bfloat16)

    sent = mixed(jnp.where((doc == first[0])[:, :, None], quer, zero), grad, "bta,btc->ac")
    pieces = exchange(sent, first[0], -1)
    back = jnp.where(visible, mixed(grad, value, "btc,bsc->bts"), 0.0).astype(jnp.bfloat16)
    grad_query = mixed(back, key, "bts,bsa->bta") + jnp.where(
        first_rows, mixed(grad, carry, "btc,bac->bta"), 0.0
    )
    own = mixed(jnp.where(first_rows, quer, zero), grad, "bta,btc->bac")
    state = arriving(pieces, last[-1])
    carries = [state]
    for b in range(SUB - 2, -1, -1):
        state = own[b + 1] + jnp.where(first[b + 1] == last[b + 1], state, 0.0)
        state = jnp.where(first[b + 1] == last[b], state, 0.0)
        carries.append(state)
    carry = jnp.stack(carries[::-1]).astype(jnp.bfloat16)
    grad_keys = mixed(back, quer, "bts,bta->bsa") + jnp.where(
        last_rows, mixed(value, carry, "bsc,bac->bsa"), 0.0
    )
    grad_values = mixed(attn, grad, "bts,btc->bsc") + jnp.where(
        last_rows, mixed(key, carry, "bsa,bac->bsc"), 0.0
    )

    rows = jnp.concatenate([grad_query, grad_keys, grad_values], -1).astype(jnp.bfloat16)
    rows = rows.reshape(SUB * tok_rows, 3 * HS)
    slots = SUB * capacity
    place = slot[None, :] == jnp.arange(seq_count * slots)[:, None]
    packed = jnp.dot(
        place.astype(jnp.bfloat16), rows, preferred_element_type=jnp.float32
    ).astype(jnp.bfloat16)
    index = lax.all_to_all(row_index, "seq", 0, 0, tiled=True)
    received = lax.all_to_all(
        packed.reshape(seq_count, slots, 3 * HS), "seq", 0, 0, tiled=True
    )
    received = received.reshape(seq_count // SUB, SUB, slots, 3, HS)
    choose = index.reshape(-1)[None, :] == jnp.arange(tok_rows)[:, None]
    choose = choose.astype(jnp.bfloat16).reshape(tok_rows, seq_count // SUB, slots)
    return mixed(choose, received, "rgk,gskjd->rjsd").astype(jnp.bfloat16).reshape(
        tok_rows, 3, width
    )


def solution(mesh):
    placed = (
        P("seq", "head"),
        P("seq", "head"),
        P("seq", "head"),
        P("seq", "head"),
        P("head"),
        P("seq"),
        P("seq"),
    )
    return jax.shard_map(
        local, mesh=mesh, in_specs=placed, out_specs=P("seq", None, "head"), check_vma=False
    )
```

```python
import jax
import jax.numpy as jnp
from jax import lax
from jax.sharding import PartitionSpec as P

HEADS = 32
HS = 128
EPSILON = 1e-05
SUB = 4
EXTRA = 16


def mixed(left, right, form):
    return jnp.einsum(form, left, right, preferred_element_type=jnp.float32)


def heads_first(array):
    return jnp.stack([array[:, at : at + HS] for at in range(0, array.shape[1], HS)])


def together(*values):
    return lax.optimization_barrier(values)


def local(query, keys, values, grad_normed, norm_gain, doc_ids, home):
    tok_rows, width = query.shape
    full_width = HEADS * HS
    seq_count = lax.axis_size("seq")
    head_count = lax.axis_size("head")
    capacity = 2 * tok_rows // seq_count
    slots = SUB * capacity
    groups = [[g * SUB + s for s in range(SUB)] for g in range(seq_count // SUB)]
    wide_groups = [[i * head_count + h for i in one for h in range(head_count)] for one in groups]
    places = jnp.arange(tok_rows)
    blocks = jnp.arange(SUB)

    owner = home // tok_rows
    target_row = home % tok_rows
    same_owner = owner[:, None] == owner[None, :]
    ranks = jnp.sum(jnp.where(same_owner & (places[:, None] < places[None, :]), 1, 0), axis=0)
    local_slot = owner * capacity + ranks
    slot_match = local_slot[None, :] == jnp.arange(seq_count * capacity)[:, None]
    row_index = jnp.max(jnp.where(slot_match, target_row[None, :], -1), axis=1)
    row_index = row_index.reshape(seq_count, capacity)

    def regroup(array):
        return lax.all_to_all(array, "seq", 0, 0, tiled=True, axis_index_groups=groups)

    later = places[:, None] >= places[None, :]
    last_row = jnp.max(jnp.where(later, doc_ids[:, None], -1), axis=0)
    first_row = jnp.min(jnp.where(later, tok_rows, doc_ids[:, None]), axis=0, initial=tok_rows)
    first_row = jnp.minimum(first_row, doc_ids)
    small = jnp.stack([doc_ids, owner, ranks, first_row, last_row]).astype(jnp.bfloat16)
    small = jnp.pad(small, ((0, EXTRA - 5), (0, 0)))
    small = jnp.broadcast_to(small[None], (SUB, EXTRA, tok_rows))
    key_value = regroup(jnp.concatenate([heads_first(keys), heads_first(values), small], axis=1))
    key = key_value[:, :tok_rows]
    value = key_value[:, tok_rows : 2 * tok_rows]
    small = key_value[:, 2 * tok_rows :].astype(jnp.float32)
    doc = small[:, 0]
    gain = norm_gain.reshape(SUB, HS)
    gain = jnp.sum(jnp.where((blocks == lax.axis_index("seq") % SUB)[:, None], gain, 0.0), axis=0)

    first, last = small[:, 3], small[:, 4]
    first_rows = (doc == first)[:, :, None]
    last_rows = (doc == last)[:, :, None]
    zero = jnp.zeros((), jnp.bfloat16)

    def exchange(state, number, sign):
        number = jnp.broadcast_to(number.astype(jnp.bfloat16), (EXTRA, HS))
        payload = jnp.concatenate([state.astype(jnp.bfloat16), number], axis=0)
        pieces = []
        for far in (1, 2):
            step = sign * far * SUB
            pairs = [(i, i + step) for i in range(seq_count) if 0 <= i + step < seq_count]
            pieces.append(lax.ppermute(payload, "seq", pairs))
        return pieces

    def entering(pieces, own, numbers, own_numbers, order):
        state = sum(
            jnp.where(
                p[HS : HS + 1].astype(jnp.float32)[None] == numbers[:, None],
                p[:HS].astype(jnp.float32)[None],
                0.0,
            )
            for p in pieces
        )
        joined = order[:, :, None] & (numbers[:, None] == own_numbers[None, :])
        inside = jnp.sum(jnp.where(joined[:, :, None], own[None], 0.0), axis=1)
        return (state + inside).astype(jnp.bfloat16)

    sent = mixed(jnp.where((doc == last[SUB - 1])[:, :, None], key, zero), value, "bta,btc->ac")
    pieces = exchange(sent, last[SUB - 1], 1)
    own = mixed(jnp.where(last_rows, key, zero), value, "bta,btc->bac")
    query_grad = jnp.concatenate([heads_first(query), heads_first(grad_normed)], axis=1)
    query_grad, own = together(query_grad, own)
    query_grad = regroup(query_grad)
    quer = query_grad[:, :tok_rows]
    normed = query_grad[:, tok_rows:]
    visible = (doc[:, :, None] == doc[:, None, :]) & (places[:, None] >= places[None, :])
    attn = jnp.where(visible, mixed(quer, key, "bta,bsa->bts"), 0.0).astype(jnp.bfloat16)
    carry = entering(pieces, own, first, last, blocks[:, None] > blocks[None, :])
    output = mixed(attn, value, "bts,bsc->btc") + jnp.where(
        first_rows, mixed(quer, carry, "bta,bac->btc"), 0.0
    )
    scaled = gain * normed.astype(jnp.float32)
    sums = jnp.concatenate([jnp.sum(output * output, -1), jnp.sum(scaled * output, -1)])
    sums = jnp.broadcast_to(sums[None], (SUB * head_count, 2 * SUB, tok_rows))
    sums = lax.all_to_all(
        sums, ("seq", "head"), 0, 0, tiled=True, axis_index_groups=wide_groups
    ).sum(0)
    squares, inner = sums[:SUB, :, None], sums[SUB:, :, None]
    inv_rms = lax.rsqrt(squares / full_width + EPSILON)
    grad = (
        inv_rms * scaled - output * (inv_rms * inv_rms * inv_rms * inner / full_width)
    ).astype(jnp.bfloat16)

    sent = mixed(jnp.where((doc == first[0])[:, :, None], quer, zero), grad, "bta,btc->ac")
    pieces = exchange(sent, first[0], -1)
    back = jnp.where(visible, mixed(grad, value, "btc,bsc->bts"), 0.0).astype(jnp.bfloat16)
    grad_query = mixed(back, key, "bts,bsa->bta") + jnp.where(
        first_rows, mixed(grad, carry, "btc,bac->bta"), 0.0
    )
    grad_query = grad_query.astype(jnp.bfloat16)
    own = mixed(jnp.where(first_rows, quer, zero), grad, "bta,btc->bac")

    slot = (small[:, 1] * slots + small[:, 2] + (blocks * capacity)[:, None]).reshape(-1)
    place = slot[None, :] == jnp.arange(seq_count * slots)[:, None].astype(jnp.float32)
    row_index, grad_query = together(row_index, grad_query)
    index = lax.all_to_all(row_index, "seq", 0, 0, tiled=True)
    choose = index.reshape(-1)[None, :] == places[:, None]
    choose = choose.astype(jnp.bfloat16).reshape(tok_rows, seq_count // SUB, slots)

    carry = entering(pieces, own, last, first, blocks[:, None] < blocks[None, :])
    grad_keys = mixed(back, quer, "bts,bta->bsa") + jnp.where(
        last_rows, mixed(value, carry, "bsc,bac->bsa"), 0.0
    )
    grad_values = mixed(attn, grad, "bts,btc->bsc") + jnp.where(
        last_rows, mixed(key, carry, "bsa,bac->bsc"), 0.0
    )
    rows = jnp.concatenate(
        [grad_query, grad_keys.astype(jnp.bfloat16), grad_values.astype(jnp.bfloat16)], -1
    )
    rows = rows.reshape(SUB * tok_rows, 3 * HS)
    packed = jnp.dot(
        place.astype(jnp.bfloat16), rows, preferred_element_type=jnp.float32
    ).astype(jnp.bfloat16)
    packed, choose = together(packed, choose)
    received = lax.all_to_all(
        packed.reshape(seq_count, slots, 3 * HS), "seq", 0, 0, tiled=True
    )
    received = received.reshape(seq_count // SUB, SUB, slots, 3, HS)
    return mixed(choose, received, "rgk,gskjd->rjsd").astype(jnp.bfloat16).reshape(
        tok_rows, 3, width
    )


def solution(mesh):
    placed = (
        P("seq", "head"),
        P("seq", "head"),
        P("seq", "head"),
        P("seq", "head"),
        P("head"),
        P("seq"),
        P("seq"),
    )
    return jax.shard_map(
        local, mesh=mesh, in_specs=placed, out_specs=P("seq", None, "head"), check_vma=False
    )
```

```python
import jax
import jax.numpy as jnp
from jax import lax
from jax.sharding import PartitionSpec as P

HEADS = 32
HS = 128
EPSILON = 1e-05
SUB = 4
WIDE = 32
EXTRA = 16


def mixed(left, right, form):
    return jnp.einsum(form, left, right, preferred_element_type=jnp.float32)


def heads_first(array):
    return jnp.stack([array[:, at : at + HS] for at in range(0, array.shape[1], HS)])


def together(*values):
    return lax.optimization_barrier(values)


def local(query, keys, values, grad_normed, norm_gain, doc_ids, home):
    tok_rows, width = query.shape
    full_width = HEADS * HS
    seq_count = lax.axis_size("seq")
    head_count = lax.axis_size("head")
    capacity = 2 * tok_rows // seq_count
    slots = SUB * capacity
    groups = [[g * SUB + s for s in range(SUB)] for g in range(seq_count // SUB)]
    wide_groups = [[i * head_count + h for i in one for h in range(head_count)] for one in groups]
    places = jnp.arange(tok_rows)
    blocks = jnp.arange(SUB)

    owner = home // tok_rows
    same_owner = owner[:, None] == owner[None, :]
    ranks = jnp.sum(jnp.where(same_owner & (places[:, None] < places[None, :]), 1, 0), axis=0)
    (homes,) = together(jnp.broadcast_to(home[None], (WIDE, tok_rows)))
    homes = lax.all_gather(homes, "seq")

    def regroup(array):
        return lax.all_to_all(array, "seq", 0, 0, tiled=True, axis_index_groups=groups)

    later = places[:, None] >= places[None, :]
    last_row = jnp.max(jnp.where(later, doc_ids[:, None], -1), axis=0)
    first_row = jnp.min(jnp.where(later, tok_rows, doc_ids[:, None]), axis=0, initial=tok_rows)
    first_row = jnp.minimum(first_row, doc_ids)
    small = jnp.stack([doc_ids, owner, ranks, first_row, last_row]).astype(jnp.bfloat16)
    small = jnp.pad(small, ((0, EXTRA - 5), (0, 0)))
    small = jnp.broadcast_to(small[None], (SUB, EXTRA, tok_rows))
    key_value = regroup(jnp.concatenate([heads_first(keys), heads_first(values), small], axis=1))
    key = key_value[:, :tok_rows]
    value = key_value[:, tok_rows : 2 * tok_rows]
    small = key_value[:, 2 * tok_rows :].astype(jnp.float32)
    doc = small[:, 0]
    gain = norm_gain.reshape(SUB, HS)
    gain = jnp.sum(jnp.where((blocks == lax.axis_index("seq") % SUB)[:, None], gain, 0.0), axis=0)

    first, last = small[:, 3], small[:, 4]
    first_rows = (doc == first)[:, :, None]
    last_rows = (doc == last)[:, :, None]
    zero = jnp.zeros((), jnp.bfloat16)

    def exchange(state, number, sign):
        number = jnp.broadcast_to(number.astype(jnp.bfloat16), (EXTRA, HS))
        payload = jnp.concatenate([state.astype(jnp.bfloat16), number], axis=0)
        pieces = []
        for far in (1, 2):
            step = sign * far * SUB
            pairs = [(i, i + step) for i in range(seq_count) if 0 <= i + step < seq_count]
            pieces.append(lax.ppermute(payload, "seq", pairs))
        return pieces

    def entering(pieces, own, numbers, own_numbers, order):
        state = sum(
            jnp.where(
                p[HS : HS + 1].astype(jnp.float32)[None] == numbers[:, None],
                p[:HS].astype(jnp.float32)[None],
                0.0,
            )
            for p in pieces
        )
        joined = order[:, :, None] & (numbers[:, None] == own_numbers[None, :])
        inside = jnp.sum(jnp.where(joined[:, :, None], own[None], 0.0), axis=1)
        return (state + inside).astype(jnp.bfloat16)

    sent = mixed(jnp.where((doc == last[SUB - 1])[:, :, None], key, zero), value, "bta,btc->ac")
    pieces = exchange(sent, last[SUB - 1], 1)
    own = mixed(jnp.where(last_rows, key, zero), value, "bta,btc->bac")
    query_grad = jnp.concatenate([heads_first(query), heads_first(grad_normed)], axis=1)
    query_grad, own = together(query_grad, own)
    query_grad = regroup(query_grad)
    quer = query_grad[:, :tok_rows]
    normed = query_grad[:, tok_rows:]
    visible = (doc[:, :, None] == doc[:, None, :]) & (places[:, None] >= places[None, :])
    attn = jnp.where(visible, mixed(quer, key, "bta,bsa->bts"), 0.0).astype(jnp.bfloat16)
    carry = entering(pieces, own, first, last, blocks[:, None] > blocks[None, :])
    output = mixed(attn, value, "bts,bsc->btc") + jnp.where(
        first_rows, mixed(quer, carry, "bta,bac->btc"), 0.0
    )
    scaled = gain * normed.astype(jnp.float32)
    sums = jnp.concatenate([jnp.sum(output * output, -1), jnp.sum(scaled * output, -1)])
    sums = jnp.broadcast_to(sums[None], (SUB * head_count, 2 * SUB, tok_rows))
    sums = lax.all_to_all(
        sums, ("seq", "head"), 0, 0, tiled=True, axis_index_groups=wide_groups
    ).sum(0)
    squares, inner = sums[:SUB, :, None], sums[SUB:, :, None]
    inv_rms = lax.rsqrt(squares / full_width + EPSILON)
    grad = (
        inv_rms * scaled - output * (inv_rms * inv_rms * inv_rms * inner / full_width)
    ).astype(jnp.bfloat16)

    sent = mixed(jnp.where((doc == first[0])[:, :, None], quer, zero), grad, "bta,btc->ac")
    pieces = exchange(sent, first[0], -1)
    back = jnp.where(visible, mixed(grad, value, "btc,bsc->bts"), 0.0).astype(jnp.bfloat16)
    grad_query = mixed(back, key, "bts,bsa->bta") + jnp.where(
        first_rows, mixed(grad, carry, "btc,bac->bta"), 0.0
    )
    grad_query = grad_query.astype(jnp.bfloat16)
    own = mixed(jnp.where(first_rows, quer, zero), grad, "bta,btc->bac")

    slot = (small[:, 1] * slots + small[:, 2] + (blocks * capacity)[:, None]).reshape(-1)
    place = slot[None, :] == jnp.arange(seq_count * slots)[:, None].astype(jnp.float32)
    (homes,) = together(homes)
    homes = homes[:, 0]
    to_me = homes // tok_rows == lax.axis_index("seq")
    order = jnp.dot(
        to_me.astype(jnp.bfloat16),
        (places[:, None] < places[None, :]).astype(jnp.bfloat16),
        preferred_element_type=jnp.float32,
    )
    taken = to_me[:, None] & (order[:, None] == jnp.arange(capacity)[:, None].astype(jnp.float32))
    index = jnp.max(jnp.where(taken, (homes % tok_rows)[:, None], -1), axis=-1)
    choose = index.reshape(-1)[None, :] == places[:, None]
    choose = choose.astype(jnp.bfloat16).reshape(tok_rows, seq_count // SUB, slots)

    carry = entering(pieces, own, last, first, blocks[:, None] < blocks[None, :])
    grad_keys = mixed(back, quer, "bts,bta->bsa") + jnp.where(
        last_rows, mixed(value, carry, "bsc,bac->bsa"), 0.0
    )
    grad_values = mixed(attn, grad, "bts,btc->bsc") + jnp.where(
        last_rows, mixed(key, carry, "bsa,bac->bsc"), 0.0
    )
    rows = jnp.concatenate(
        [grad_query, grad_keys.astype(jnp.bfloat16), grad_values.astype(jnp.bfloat16)], -1
    )
    rows = rows.reshape(SUB * tok_rows, 3 * HS)
    packed = jnp.dot(
        place.astype(jnp.bfloat16), rows, preferred_element_type=jnp.float32
    ).astype(jnp.bfloat16)
    packed, choose = together(packed, choose)
    received = lax.all_to_all(
        packed.reshape(seq_count, slots, 3 * HS), "seq", 0, 0, tiled=True
    )
    received = received.reshape(seq_count // SUB, SUB, slots, 3, HS)
    return mixed(choose, received, "rgk,gskjd->rjsd").astype(jnp.bfloat16).reshape(
        tok_rows, 3, width
    )


def solution(mesh):
    placed = (
        P("seq", "head"),
        P("seq", "head"),
        P("seq", "head"),
        P("seq", "head"),
        P("head"),
        P("seq"),
        P("seq"),
    )
    return jax.shard_map(
        local, mesh=mesh, in_specs=placed, out_specs=P("seq", None, "head"), check_vma=False
    )
```

```python
import jax
import jax.numpy as jnp
from jax import lax
from jax.sharding import PartitionSpec as P

HEADS = 32
HS = 128
EPSILON = 1e-05
SUB = 4
EXTRA = 16


def mixed(left, right, form):
    return jnp.einsum(form, left, right, preferred_element_type=jnp.float32)


def heads_first(array):
    return jnp.stack([array[:, at : at + HS] for at in range(0, array.shape[1], HS)])


def together(*values):
    return lax.optimization_barrier(values)


def local(query, keys, values, grad_normed, norm_gain, doc_ids, home):
    tok_rows, width = query.shape
    full_width = HEADS * HS
    seq_count = lax.axis_size("seq")
    head_count = lax.axis_size("head")
    capacity = 2 * tok_rows // seq_count
    slots = SUB * capacity
    groups = [[g * SUB + s for s in range(SUB)] for g in range(seq_count // SUB)]
    wide_groups = [[i * head_count + h for i in one for h in range(head_count)] for one in groups]
    places = jnp.arange(tok_rows)
    blocks = jnp.arange(SUB)

    owner = home // tok_rows
    target_row = home % tok_rows
    same_owner = owner[:, None] == owner[None, :]
    ranks = jnp.sum(jnp.where(same_owner & (places[:, None] < places[None, :]), 1, 0), axis=0)

    def regroup(array):
        return lax.all_to_all(array, "seq", 0, 0, tiled=True, axis_index_groups=groups)

    later = places[:, None] >= places[None, :]
    last_row = jnp.max(jnp.where(later, doc_ids[:, None], -1), axis=0)
    first_row = jnp.min(jnp.where(later, tok_rows, doc_ids[:, None]), axis=0, initial=tok_rows)
    first_row = jnp.minimum(first_row, doc_ids)
    small = jnp.stack([doc_ids, owner, ranks, first_row, last_row, target_row]).astype(jnp.bfloat16)
    small = jnp.pad(small, ((0, EXTRA - 6), (0, 0)))
    small = jnp.broadcast_to(small[None], (SUB, EXTRA, tok_rows))
    key_value = regroup(jnp.concatenate([heads_first(keys), heads_first(values), small], axis=1))
    key = key_value[:, :tok_rows]
    value = key_value[:, tok_rows : 2 * tok_rows]
    small = key_value[:, 2 * tok_rows :].astype(jnp.float32)
    doc = small[:, 0]
    gain = norm_gain.reshape(SUB, HS)
    gain = jnp.sum(jnp.where((blocks == lax.axis_index("seq") % SUB)[:, None], gain, 0.0), axis=0)

    first, last = small[:, 3], small[:, 4]
    first_rows = (doc == first)[:, :, None]
    last_rows = (doc == last)[:, :, None]
    zero = jnp.zeros((), jnp.bfloat16)

    def exchange(state, number, sign):
        number = jnp.broadcast_to(number.astype(jnp.bfloat16), (EXTRA, HS))
        payload = jnp.concatenate([state.astype(jnp.bfloat16), number], axis=0)
        pieces = []
        for far in (1, 2):
            step = sign * far * SUB
            pairs = [(i, i + step) for i in range(seq_count) if 0 <= i + step < seq_count]
            pieces.append(lax.ppermute(payload, "seq", pairs))
        return pieces

    def entering(pieces, own, numbers, own_numbers, order):
        state = sum(
            jnp.where(
                p[HS : HS + 1].astype(jnp.float32)[None] == numbers[:, None],
                p[:HS].astype(jnp.float32)[None],
                0.0,
            )
            for p in pieces
        )
        joined = order[:, :, None] & (numbers[:, None] == own_numbers[None, :])
        inside = jnp.sum(jnp.where(joined[:, :, None], own[None], 0.0), axis=1)
        return (state + inside).astype(jnp.bfloat16)

    sent = mixed(jnp.where((doc == last[SUB - 1])[:, :, None], key, zero), value, "bta,btc->ac")
    pieces = exchange(sent, last[SUB - 1], 1)
    own = mixed(jnp.where(last_rows, key, zero), value, "bta,btc->bac")
    query_grad = jnp.concatenate([heads_first(query), heads_first(grad_normed)], axis=1)
    query_grad, own = together(query_grad, own)
    query_grad = regroup(query_grad)
    quer = query_grad[:, :tok_rows]
    normed = query_grad[:, tok_rows:]
    visible = (doc[:, :, None] == doc[:, None, :]) & (places[:, None] >= places[None, :])
    attn = jnp.where(visible, mixed(quer, key, "bta,bsa->bts"), 0.0).astype(jnp.bfloat16)
    carry = entering(pieces, own, first, last, blocks[:, None] > blocks[None, :])
    output = mixed(attn, value, "bts,bsc->btc") + jnp.where(
        first_rows, mixed(quer, carry, "bta,bac->btc"), 0.0
    )
    scaled = gain * normed.astype(jnp.float32)
    sums = jnp.concatenate([jnp.sum(output * output, -1), jnp.sum(scaled * output, -1)])
    sums = jnp.broadcast_to(sums[None], (SUB * head_count, 2 * SUB, tok_rows))
    sums = lax.all_to_all(
        sums, ("seq", "head"), 0, 0, tiled=True, axis_index_groups=wide_groups
    ).sum(0)
    squares, inner = sums[:SUB, :, None], sums[SUB:, :, None]
    inv_rms = lax.rsqrt(squares / full_width + EPSILON)
    grad = (
        inv_rms * scaled - output * (inv_rms * inv_rms * inv_rms * inner / full_width)
    ).astype(jnp.bfloat16)

    sent = mixed(jnp.where((doc == first[0])[:, :, None], quer, zero), grad, "bta,btc->ac")
    pieces = exchange(sent, first[0], -1)
    back = jnp.where(visible, mixed(grad, value, "btc,bsc->bts"), 0.0).astype(jnp.bfloat16)
    grad_query = mixed(back, key, "bts,bsa->bta") + jnp.where(
        first_rows, mixed(grad, carry, "btc,bac->bta"), 0.0
    )
    grad_query = grad_query.astype(jnp.bfloat16)
    own = mixed(jnp.where(first_rows, quer, zero), grad, "bta,btc->bac")

    slot = (small[:, 1] * slots + small[:, 2] + (blocks * capacity)[:, None]).reshape(-1)
    place = slot[None, :] == jnp.arange(seq_count * slots)[:, None].astype(jnp.float32)
    peers = [[g * SUB + s for g in range(seq_count // SUB)] for s in range(SUB)]
    peer_slot = jnp.arange(seq_count // SUB)[:, None] * SUB + lax.axis_index("seq") % SUB
    peer_slot = (peer_slot * slots + jnp.arange(slots)[None, :]).astype(jnp.float32)
    row = small[:, 5].reshape(-1)
    row_index = jnp.max(jnp.where(slot == peer_slot[:, :, None], row, -1.0), axis=-1)
    row_index, grad_query = together(row_index[:, None], grad_query)
    index = lax.all_to_all(row_index, "seq", 0, 0, tiled=True, axis_index_groups=peers)[:, 0]
    choose = (index[None] == places[:, None, None].astype(jnp.float32)).astype(jnp.bfloat16)

    carry = entering(pieces, own, last, first, blocks[:, None] < blocks[None, :])
    grad_keys = mixed(back, quer, "bts,bta->bsa") + jnp.where(
        last_rows, mixed(value, carry, "bsc,bac->bsa"), 0.0
    )
    grad_values = mixed(attn, grad, "bts,btc->bsc") + jnp.where(
        last_rows, mixed(key, carry, "bsa,bac->bsc"), 0.0
    )
    rows = jnp.concatenate(
        [grad_query, grad_keys.astype(jnp.bfloat16), grad_values.astype(jnp.bfloat16)], -1
    )
    rows = rows.reshape(SUB * tok_rows, 3 * HS)
    packed = jnp.dot(
        place.astype(jnp.bfloat16), rows, preferred_element_type=jnp.float32
    ).astype(jnp.bfloat16)
    packed, choose = together(packed, choose)
    received = lax.all_to_all(
        packed.reshape(seq_count, slots, 3 * HS), "seq", 0, 0, tiled=True
    )
    received = received.reshape(seq_count // SUB, SUB, slots, 3, HS)
    return mixed(choose, received, "rgk,gskjd->rjsd").astype(jnp.bfloat16).reshape(
        tok_rows, 3, width
    )


def solution(mesh):
    placed = (
        P("seq", "head"),
        P("seq", "head"),
        P("seq", "head"),
        P("seq", "head"),
        P("head"),
        P("seq"),
        P("seq"),
    )
    return jax.shard_map(
        local, mesh=mesh, in_specs=placed, out_specs=P("seq", None, "head"), check_vma=False
    )
```

```python
import jax
import jax.numpy as jnp
from jax import lax
from jax.sharding import PartitionSpec as P

HEADS = 32
HS = 128
EPSILON = 1e-05
SUB = 4
EXTRA = 16


def mixed(left, right, form):
    return jnp.einsum(form, left, right, preferred_element_type=jnp.float32)


def heads_first(array):
    return jnp.stack([array[:, at : at + HS] for at in range(0, array.shape[1], HS)])


def together(*values):
    return lax.optimization_barrier(values)


def local(query, keys, values, grad_normed, norm_gain, doc_ids, home):
    tok_rows, width = query.shape
    full_width = HEADS * HS
    seq_count = lax.axis_size("seq")
    head_count = lax.axis_size("head")
    capacity = 2 * tok_rows // seq_count
    slots = SUB * capacity
    groups = [[g * SUB + s for s in range(SUB)] for g in range(seq_count // SUB)]
    wide_groups = [[i * head_count + h for i in one for h in range(head_count)] for one in groups]
    places = jnp.arange(tok_rows)
    blocks = jnp.arange(SUB)

    owner = home // tok_rows
    target_row = home % tok_rows
    same_owner = owner[:, None] == owner[None, :]
    ranks = jnp.sum(jnp.where(same_owner & (places[:, None] < places[None, :]), 1, 0), axis=0)

    def regroup(array):
        return lax.all_to_all(array, "seq", 0, 0, tiled=True, axis_index_groups=groups)

    later = places[:, None] >= places[None, :]
    last_row = jnp.max(jnp.where(later, doc_ids[:, None], -1), axis=0)
    first_row = jnp.min(jnp.where(later, tok_rows, doc_ids[:, None]), axis=0, initial=tok_rows)
    first_row = jnp.minimum(first_row, doc_ids)
    small = jnp.stack([doc_ids, owner, ranks, first_row, last_row, target_row]).astype(jnp.bfloat16)
    small = jnp.pad(small, ((0, EXTRA - 6), (0, 0)))
    small = jnp.broadcast_to(small[None], (SUB, EXTRA, tok_rows))
    key_value = regroup(jnp.concatenate([heads_first(keys), heads_first(values), small], axis=1))
    key = key_value[:, :tok_rows]
    value = key_value[:, tok_rows : 2 * tok_rows]
    small = key_value[:, 2 * tok_rows :].astype(jnp.float32)
    doc = small[:, 0]
    gain = norm_gain.reshape(SUB, HS)
    gain = jnp.sum(jnp.where((blocks == lax.axis_index("seq") % SUB)[:, None], gain, 0.0), axis=0)

    first, last = small[:, 3], small[:, 4]
    first_rows = (doc == first)[:, :, None]
    last_rows = (doc == last)[:, :, None]
    zero = jnp.zeros((), jnp.bfloat16)

    def exchange(state, number, sign):
        number = jnp.broadcast_to(number.astype(jnp.bfloat16), (EXTRA, HS))
        payload = jnp.concatenate([state.astype(jnp.bfloat16), number], axis=0)
        pieces = []
        for far in (1, 2):
            step = sign * far * SUB
            pairs = [(i, i + step) for i in range(seq_count) if 0 <= i + step < seq_count]
            pieces.append(lax.ppermute(payload, "seq", pairs))
        return pieces

    def entering(pieces, own, numbers, own_numbers, order):
        state = sum(
            jnp.where(
                p[HS : HS + 1].astype(jnp.float32)[None] == numbers[:, None],
                p[:HS].astype(jnp.float32)[None],
                0.0,
            )
            for p in pieces
        )
        joined = order[:, :, None] & (numbers[:, None] == own_numbers[None, :])
        inside = jnp.sum(jnp.where(joined[:, :, None], own[None], 0.0), axis=1)
        return (state + inside).astype(jnp.bfloat16)

    sent = mixed(jnp.where((doc == last[SUB - 1])[:, :, None], key, zero), value, "bta,btc->ac")
    pieces = exchange(sent, last[SUB - 1], 1)
    own = mixed(jnp.where(last_rows, key, zero), value, "bta,btc->bac")
    query_grad = jnp.concatenate([heads_first(query), heads_first(grad_normed)], axis=1)
    query_grad, own = together(query_grad, own)
    query_grad = regroup(query_grad)
    quer = query_grad[:, :tok_rows]
    normed = query_grad[:, tok_rows:]
    visible = (doc[:, :, None] == doc[:, None, :]) & (places[:, None] >= places[None, :])
    attn = jnp.where(visible, mixed(quer, key, "bta,bsa->bts"), 0.0).astype(jnp.bfloat16)
    carry = entering(pieces, own, first, last, blocks[:, None] > blocks[None, :])
    output = mixed(attn, value, "bts,bsc->btc") + jnp.where(
        first_rows, mixed(quer, carry, "bta,bac->btc"), 0.0
    )
    scaled = gain * normed.astype(jnp.float32)
    sums = jnp.concatenate([jnp.sum(output * output, -1), jnp.sum(scaled * output, -1)])
    sums = jnp.broadcast_to(sums[None], (SUB * head_count, 2 * SUB, tok_rows))
    sums = lax.all_to_all(
        sums, ("seq", "head"), 0, 0, tiled=True, axis_index_groups=wide_groups
    ).sum(0)
    squares, inner = sums[:SUB, :, None], sums[SUB:, :, None]
    inv_rms = lax.rsqrt(squares / full_width + EPSILON)
    grad = (
        inv_rms * scaled - output * (inv_rms * inv_rms * inv_rms * inner / full_width)
    ).astype(jnp.bfloat16)

    sent = mixed(jnp.where((doc == first[0])[:, :, None], quer, zero), grad, "bta,btc->ac")
    pieces = exchange(sent, first[0], -1)
    back = jnp.where(visible, mixed(grad, value, "btc,bsc->bts"), 0.0).astype(jnp.bfloat16)
    grad_query = mixed(back, key, "bts,bsa->bta") + jnp.where(
        first_rows, mixed(grad, carry, "btc,bac->bta"), 0.0
    )
    grad_query = grad_query.astype(jnp.bfloat16)
    own = mixed(jnp.where(first_rows, quer, zero), grad, "bta,btc->bac")

    owners, ranks, row = (small[:, at].reshape(-1) for at in (1, 2, 5))
    rank_slot = (small[:, 2] + (blocks * capacity)[:, None]).reshape(-1)
    slot = owners * slots + rank_slot
    place = slot[None, :] == jnp.arange(seq_count * slots)[:, None].astype(jnp.float32)
    to_owner = owners[None, :] == jnp.arange(seq_count)[:, None].astype(jnp.float32)
    at_slot = rank_slot[:, None] == jnp.arange(HS)[None, :].astype(jnp.float32)
    index = jnp.dot(
        to_owner.astype(jnp.bfloat16),
        jnp.where(at_slot, row[:, None] + 1.0, 0.0).astype(jnp.bfloat16),
        preferred_element_type=jnp.float32,
    ).astype(jnp.bfloat16)
    index = jnp.pad(index[:, None, None], ((0, 0), (0, 0), (0, 1), (0, 0)))
    index, grad_query = together(index, grad_query)

    carry = entering(pieces, own, last, first, blocks[:, None] < blocks[None, :])
    grad_keys = mixed(back, quer, "bts,bta->bsa") + jnp.where(
        last_rows, mixed(value, carry, "bsc,bac->bsa"), 0.0
    )
    grad_values = mixed(attn, grad, "bts,btc->bsc") + jnp.where(
        last_rows, mixed(key, carry, "bsa,bac->bsc"), 0.0
    )
    rows = jnp.concatenate(
        [grad_query, grad_keys.astype(jnp.bfloat16), grad_values.astype(jnp.bfloat16)], -1
    )
    rows = rows.reshape(SUB * tok_rows, 3 * HS)
    packed = jnp.dot(
        place.astype(jnp.bfloat16), rows, preferred_element_type=jnp.float32
    ).astype(jnp.bfloat16)
    halves = slots // 8
    packed = packed.reshape(seq_count, halves, 8, 3, HS).transpose(0, 1, 3, 2, 4)
    packed = packed.reshape(seq_count, halves * 12, 2, HS)
    packed = jnp.concatenate([packed, index], axis=1)
    packed, numbers = together(packed, (places + 1).astype(jnp.float32))
    received = lax.all_to_all(packed, "seq", 0, 0, tiled=True)
    index = received[::SUB, halves * 12, 0, :slots].astype(jnp.float32)
    choose = (index[None] == numbers[:, None, None]).astype(jnp.bfloat16)
    choose = choose.reshape(tok_rows, seq_count // SUB, halves, 8)
    received = received[:, : halves * 12].reshape(seq_count // SUB, SUB, halves, 3, 8, HS)
    return mixed(choose, received, "rghk,gshjkd->rjsd").astype(jnp.bfloat16).reshape(
        tok_rows, 3, width
    )


def solution(mesh):
    placed = (
        P("seq", "head"),
        P("seq", "head"),
        P("seq", "head"),
        P("seq", "head"),
        P("head"),
        P("seq"),
        P("seq"),
    )
    return jax.shard_map(
        local, mesh=mesh, in_specs=placed, out_specs=P("seq", None, "head"), check_vma=False
    )
```

```python
import jax
import jax.numpy as jnp
from jax import lax
from jax.experimental import pallas as pl
from jax.experimental.pallas import tpu as pltpu
from jax.sharding import PartitionSpec as P

HEADS = 32
HS = 128
EPSILON = 1e-05
SUB = 4
EXTRA = 8


def mixed(left, right, form):
    return jnp.einsum(form, left, right, preferred_element_type=jnp.float32)


def heads_first(array):
    return jnp.stack([array[:, at : at + HS] for at in range(0, array.shape[1], HS)])


def prepare(key_ref, value_ref, doc_ref, home_ref, out_ref):
    tok_rows = key_ref.shape[0]
    for s in range(SUB):
        out_ref[s, :tok_rows] = key_ref[:, s * HS : (s + 1) * HS]
        out_ref[s, tok_rows : 2 * tok_rows] = value_ref[:, s * HS : (s + 1) * HS]
    doc = doc_ref[...].astype(jnp.float32)
    home = home_ref[...]
    owner = lax.shift_right_logical(home, tok_rows.bit_length() - 1).astype(jnp.float32)
    target_row = (home & (tok_rows - 1)).astype(jnp.float32)
    across = jnp.broadcast_to(owner, (tok_rows, tok_rows))
    above = lax.broadcasted_iota(jnp.int32, across.shape, 0)
    along = lax.broadcasted_iota(jnp.int32, across.shape, 1)
    earlier = (across == across.T) & (above < along)
    ranks = jnp.sum(jnp.where(earlier, 1.0, 0.0), axis=0, keepdims=True)
    first = jnp.min(doc, axis=1, keepdims=True)
    last = jnp.max(doc, axis=1, keepdims=True)
    line = lax.broadcasted_iota(jnp.int32, (EXTRA, tok_rows), 0)
    small = jnp.zeros((EXTRA, tok_rows), jnp.float32)
    for at, value in enumerate((doc, owner, ranks, first, last, target_row)):
        small = jnp.where(line == at, value, small)
    for s in range(SUB):
        out_ref[s, 2 * tok_rows :] = small.astype(jnp.bfloat16)


def together(*values):
    return lax.optimization_barrier(values)


def local(query, keys, values, grad_normed, norm_gain, doc_ids, home):
    tok_rows, width = query.shape
    full_width = HEADS * HS
    seq_count = lax.axis_size("seq")
    head_count = lax.axis_size("head")
    capacity = 2 * tok_rows // seq_count
    slots = SUB * capacity
    groups = [[g * SUB + s for s in range(SUB)] for g in range(seq_count // SUB)]
    wide_groups = [[i * head_count + h for i in one for h in range(head_count)] for one in groups]
    places = jnp.arange(tok_rows)
    blocks = jnp.arange(SUB)

    def regroup(array):
        return lax.all_to_all(array, "seq", 0, 0, tiled=True, axis_index_groups=groups)

    key_value = pl.pallas_call(
        prepare,
        out_shape=jax.ShapeDtypeStruct((SUB, 2 * tok_rows + EXTRA, HS), jnp.bfloat16),
        in_specs=[pl.BlockSpec(memory_space=pltpu.VMEM)] * 4,
        out_specs=pl.BlockSpec(memory_space=pltpu.VMEM),
    )(keys, values, doc_ids.reshape(1, -1), home.reshape(1, -1))
    key_value = regroup(key_value)
    key = key_value[:, :tok_rows]
    value = key_value[:, tok_rows : 2 * tok_rows]
    small = key_value[:, 2 * tok_rows :].astype(jnp.float32)
    doc = small[:, 0]
    gain = norm_gain.reshape(SUB, HS)
    gain = jnp.sum(jnp.where((blocks == lax.axis_index("seq") % SUB)[:, None], gain, 0.0), axis=0)

    first, last = small[:, 3], small[:, 4]
    first_rows = (doc == first)[:, :, None]
    last_rows = (doc == last)[:, :, None]
    zero = jnp.zeros((), jnp.bfloat16)

    def exchange(state, number, sign):
        number = jnp.broadcast_to(number.astype(jnp.bfloat16), (EXTRA, HS))
        payload = jnp.concatenate([state.astype(jnp.bfloat16), number], axis=0)
        pieces = []
        for far in (1, 2):
            step = sign * far * SUB
            pairs = [(i, i + step) for i in range(seq_count) if 0 <= i + step < seq_count]
            pieces.append(lax.ppermute(payload, "seq", pairs))
        return pieces

    def entering(pieces, own, numbers, own_numbers, order):
        state = sum(
            jnp.where(
                p[HS : HS + 1].astype(jnp.float32)[None] == numbers[:, None],
                p[:HS].astype(jnp.float32)[None],
                0.0,
            )
            for p in pieces
        )
        joined = order[:, :, None] & (numbers[:, None] == own_numbers[None, :])
        inside = jnp.sum(jnp.where(joined[:, :, None], own[None], 0.0), axis=1)
        return (state + inside).astype(jnp.bfloat16)

    sent = mixed(jnp.where((doc == last[SUB - 1])[:, :, None], key, zero), value, "bta,btc->ac")
    pieces = exchange(sent, last[SUB - 1], 1)
    own = mixed(jnp.where(last_rows, key, zero), value, "bta,btc->bac")
    query_grad = jnp.concatenate([heads_first(query), heads_first(grad_normed)], axis=1)
    query_grad, own = together(query_grad, own)
    query_grad = regroup(query_grad)
    quer = query_grad[:, :tok_rows]
    normed = query_grad[:, tok_rows:]
    visible = (doc[:, :, None] == doc[:, None, :]) & (places[:, None] >= places[None, :])
    attn = jnp.where(visible, mixed(quer, key, "bta,bsa->bts"), 0.0).astype(jnp.bfloat16)
    carry = entering(pieces, own, first, last, blocks[:, None] > blocks[None, :])
    output = mixed(attn, value, "bts,bsc->btc") + jnp.where(
        first_rows, mixed(quer, carry, "bta,bac->btc"), 0.0
    )
    scaled = gain * normed.astype(jnp.float32)
    sums = jnp.concatenate([jnp.sum(output * output, -1), jnp.sum(scaled * output, -1)])
    sums = jnp.broadcast_to(sums[None], (SUB * head_count, 2 * SUB, tok_rows))
    sums = lax.all_to_all(
        sums, ("seq", "head"), 0, 0, tiled=True, axis_index_groups=wide_groups
    ).sum(0)
    squares, inner = sums[:SUB, :, None], sums[SUB:, :, None]
    inv_rms = lax.rsqrt(squares / full_width + EPSILON)
    grad = (
        inv_rms * scaled - output * (inv_rms * inv_rms * inv_rms * inner / full_width)
    ).astype(jnp.bfloat16)

    sent = mixed(jnp.where((doc == first[0])[:, :, None], quer, zero), grad, "bta,btc->ac")
    pieces = exchange(sent, first[0], -1)
    back = jnp.where(visible, mixed(grad, value, "btc,bsc->bts"), 0.0).astype(jnp.bfloat16)
    grad_query = mixed(back, key, "bts,bsa->bta") + jnp.where(
        first_rows, mixed(grad, carry, "btc,bac->bta"), 0.0
    )
    grad_query = grad_query.astype(jnp.bfloat16)
    own = mixed(jnp.where(first_rows, quer, zero), grad, "bta,btc->bac")

    owners, ranks, row = (small[:, at].reshape(-1) for at in (1, 2, 5))
    rank_slot = (small[:, 2] + (blocks * capacity)[:, None]).reshape(-1)
    slot = owners * slots + rank_slot
    place = slot[None, :] == jnp.arange(seq_count * slots)[:, None].astype(jnp.float32)
    to_owner = owners[None, :] == jnp.arange(seq_count)[:, None].astype(jnp.float32)
    at_slot = rank_slot[:, None] == jnp.arange(HS)[None, :].astype(jnp.float32)
    index = jnp.dot(
        to_owner.astype(jnp.bfloat16),
        jnp.where(at_slot, row[:, None] + 1.0, 0.0).astype(jnp.bfloat16),
        preferred_element_type=jnp.float32,
    ).astype(jnp.bfloat16)
    index = jnp.pad(index[:, None, None], ((0, 0), (0, 0), (0, 1), (0, 0)))
    index, grad_query = together(index, grad_query)

    carry = entering(pieces, own, last, first, blocks[:, None] < blocks[None, :])
    grad_keys = mixed(back, quer, "bts,bta->bsa") + jnp.where(
        last_rows, mixed(value, carry, "bsc,bac->bsa"), 0.0
    )
    grad_values = mixed(attn, grad, "bts,btc->bsc") + jnp.where(
        last_rows, mixed(key, carry, "bsa,bac->bsc"), 0.0
    )
    rows = jnp.concatenate(
        [grad_query, grad_keys.astype(jnp.bfloat16), grad_values.astype(jnp.bfloat16)], -1
    )
    rows = rows.reshape(SUB * tok_rows, 3 * HS)
    packed = jnp.dot(
        place.astype(jnp.bfloat16), rows, preferred_element_type=jnp.float32
    ).astype(jnp.bfloat16)
    halves = slots // 8
    packed = packed.reshape(seq_count, halves, 8, 3, HS).transpose(0, 1, 3, 2, 4)
    packed = packed.reshape(seq_count, halves * 12, 2, HS)
    packed = jnp.concatenate([packed, index], axis=1)
    packed, numbers = together(packed, (places + 1).astype(jnp.float32))
    received = lax.all_to_all(packed, "seq", 0, 0, tiled=True)
    index = received[::SUB, halves * 12, 0, :slots].astype(jnp.float32)
    choose = (index[None] == numbers[:, None, None]).astype(jnp.bfloat16)
    choose = choose.reshape(tok_rows, seq_count // SUB, halves, 8)
    received = received[:, : halves * 12].reshape(seq_count // SUB, SUB, halves, 3, 8, HS)
    return mixed(choose, received, "rghk,gshjkd->rjsd").astype(jnp.bfloat16).reshape(
        tok_rows, 3, width
    )


def solution(mesh):
    placed = (
        P("seq", "head"),
        P("seq", "head"),
        P("seq", "head"),
        P("seq", "head"),
        P("head"),
        P("seq"),
        P("seq"),
    )
    return jax.shard_map(
        local, mesh=mesh, in_specs=placed, out_specs=P("seq", None, "head"), check_vma=False
    )
```

```python
import jax
import jax.numpy as jnp
from jax import lax
from jax.experimental import pallas as pl
from jax.experimental.pallas import tpu as pltpu
from jax.sharding import PartitionSpec as P

HEADS = 32
HS = 128
EPSILON = 1e-05
SUB = 4
EXTRA = 8


def mixed(left, right, form):
    return jnp.einsum(form, left, right, preferred_element_type=jnp.float32)


def heads_first(array):
    return jnp.stack([array[:, at : at + HS] for at in range(0, array.shape[1], HS)])


def prepare(key_ref, value_ref, doc_ref, home_ref, out_ref):
    tok_rows = key_ref.shape[0]
    for s in range(SUB):
        out_ref[s, :tok_rows] = key_ref[:, s * HS : (s + 1) * HS]
        out_ref[s, tok_rows : 2 * tok_rows] = value_ref[:, s * HS : (s + 1) * HS]
    doc = doc_ref[...].astype(jnp.float32)
    home = home_ref[...]
    owner = lax.shift_right_logical(home, tok_rows.bit_length() - 1).astype(jnp.float32)
    target_row = (home & (tok_rows - 1)).astype(jnp.float32)
    across = jnp.broadcast_to(owner, (tok_rows, tok_rows))
    above = lax.broadcasted_iota(jnp.int32, across.shape, 0)
    along = lax.broadcasted_iota(jnp.int32, across.shape, 1)
    earlier = (across == across.T) & (above < along)
    ranks = jnp.sum(jnp.where(earlier, 1.0, 0.0), axis=0, keepdims=True)
    first = jnp.min(doc, axis=1, keepdims=True)
    last = jnp.max(doc, axis=1, keepdims=True)
    line = lax.broadcasted_iota(jnp.int32, (EXTRA, tok_rows), 0)
    small = jnp.zeros((EXTRA, tok_rows), jnp.float32)
    for at, value in enumerate((doc, owner, ranks, first, last, target_row)):
        small = jnp.where(line == at, value, small)
    for s in range(SUB):
        out_ref[s, 2 * tok_rows :] = small.astype(jnp.bfloat16)


def together(*values):
    return lax.optimization_barrier(values)


def local(query, keys, values, grad_normed, norm_gain, doc_ids, home):
    tok_rows, width = query.shape
    full_width = HEADS * HS
    seq_count = lax.axis_size("seq")
    head_count = lax.axis_size("head")
    capacity = 2 * tok_rows // seq_count
    slots = SUB * capacity
    groups = [[g * SUB + s for s in range(SUB)] for g in range(seq_count // SUB)]
    wide_groups = [[i * head_count + h for i in one for h in range(head_count)] for one in groups]
    places = jnp.arange(tok_rows)
    blocks = jnp.arange(SUB)

    def regroup(array):
        return lax.all_to_all(array, "seq", 0, 0, tiled=True, axis_index_groups=groups)

    key_value = pl.pallas_call(
        prepare,
        out_shape=jax.ShapeDtypeStruct((SUB, 2 * tok_rows + EXTRA, HS), jnp.bfloat16),
        in_specs=[pl.BlockSpec(memory_space=pltpu.VMEM)] * 4,
        out_specs=pl.BlockSpec(memory_space=pltpu.VMEM),
    )(keys, values, doc_ids.reshape(1, -1), home.reshape(1, -1))
    key_value = regroup(key_value)
    key = key_value[:, :tok_rows]
    value = key_value[:, tok_rows : 2 * tok_rows]
    small = key_value[:, 2 * tok_rows :].astype(jnp.float32)
    doc = small[:, 0]
    gain = norm_gain.reshape(SUB, HS)
    gain = jnp.sum(jnp.where((blocks == lax.axis_index("seq") % SUB)[:, None], gain, 0.0), axis=0)

    first, last = small[:, 3], small[:, 4]
    first_rows = (doc == first)[:, :, None]
    last_rows = (doc == last)[:, :, None]
    zero = jnp.zeros((), jnp.bfloat16)

    def shifted(load, groups_on):
        step = groups_on * SUB
        pairs = [(i, i + step) for i in range(seq_count) if 0 <= i + step < seq_count]
        return lax.ppermute(load, "seq", pairs)

    def payload(state, number):
        number = jnp.broadcast_to(number.astype(jnp.bfloat16), (EXTRA, HS))
        return jnp.concatenate([state.astype(jnp.bfloat16), number], axis=0)

    def entering(pieces, own, numbers, own_numbers, order):
        state = sum(
            jnp.where(
                p[HS : HS + 1].astype(jnp.float32)[None] == numbers[:, None],
                p[:HS].astype(jnp.float32)[None],
                0.0,
            )
            for p in pieces
        )
        joined = order[:, :, None] & (numbers[:, None] == own_numbers[None, :])
        inside = jnp.sum(jnp.where(joined[:, :, None], own[None], 0.0), axis=1)
        return (state + inside).astype(jnp.bfloat16)

    sent = mixed(jnp.where((doc == last[SUB - 1])[:, :, None], key, zero), value, "bta,btc->ac")
    near = shifted(payload(sent, last[SUB - 1]), 1)
    pieces = [near, shifted(near, 1)]
    own = mixed(jnp.where(last_rows, key, zero), value, "bta,btc->bac")
    query_grad = jnp.concatenate([heads_first(query), heads_first(grad_normed)], axis=1)
    numbers, lanes, all_slots, all_owners, starts = (
        count.astype(jnp.float32)
        for count in (
            places + 1,
            jnp.arange(HS),
            jnp.arange(seq_count * slots),
            jnp.arange(seq_count),
            blocks * capacity,
        )
    )
    query_grad, own, numbers, lanes, all_slots, all_owners, starts = together(
        query_grad, own, numbers, lanes, all_slots, all_owners, starts
    )
    query_grad = regroup(query_grad)
    quer = query_grad[:, :tok_rows]
    normed = query_grad[:, tok_rows:]
    visible = (doc[:, :, None] == doc[:, None, :]) & (places[:, None] >= places[None, :])
    attn = jnp.where(visible, mixed(quer, key, "bta,bsa->bts"), 0.0).astype(jnp.bfloat16)
    carry = entering(pieces, own, first, last, blocks[:, None] > blocks[None, :])
    output = mixed(attn, value, "bts,bsc->btc") + jnp.where(
        first_rows, mixed(quer, carry, "bta,bac->btc"), 0.0
    )
    scaled = gain * normed.astype(jnp.float32)
    sums = jnp.concatenate([jnp.sum(output * output, -1), jnp.sum(scaled * output, -1)])
    sums = jnp.broadcast_to(sums[None], (SUB * head_count, 2 * SUB, tok_rows))
    sums = lax.all_to_all(
        sums, ("seq", "head"), 0, 0, tiled=True, axis_index_groups=wide_groups
    ).sum(0)
    squares, inner = sums[:SUB, :, None], sums[SUB:, :, None]
    inv_rms = lax.rsqrt(squares / full_width + EPSILON)
    grad = (
        inv_rms * scaled - output * (inv_rms * inv_rms * inv_rms * inner / full_width)
    ).astype(jnp.bfloat16)

    sent = mixed(jnp.where((doc == first[0])[:, :, None], quer, zero), grad, "bta,btc->ac")
    sent = payload(sent, first[0])
    pieces = [shifted(sent, -1), shifted(sent, -2)]
    back = jnp.where(visible, mixed(grad, value, "btc,bsc->bts"), 0.0).astype(jnp.bfloat16)
    grad_query = mixed(back, key, "bts,bsa->bta") + jnp.where(
        first_rows, mixed(grad, carry, "btc,bac->bta"), 0.0
    )
    grad_query = grad_query.astype(jnp.bfloat16)
    own = mixed(jnp.where(first_rows, quer, zero), grad, "bta,btc->bac")

    small, grad = together(small, grad)
    owners, ranks, row = (small[:, at].reshape(-1) for at in (1, 2, 5))
    rank_slot = (small[:, 2] + starts[:, None]).reshape(-1)
    slot = owners * slots + rank_slot
    place = slot[None, :] == all_slots[:, None]
    to_owner = owners[None, :] == all_owners[:, None]
    at_slot = rank_slot[:, None] == lanes[None, :]
    index = jnp.dot(
        to_owner.astype(jnp.bfloat16),
        jnp.where(at_slot, row[:, None] + 1.0, 0.0).astype(jnp.bfloat16),
        preferred_element_type=jnp.float32,
    ).astype(jnp.bfloat16)
    index = jnp.pad(index[:, None, None], ((0, 0), (0, 0), (0, 1), (0, 0)))
    index, place, grad_query = together(index, place.astype(jnp.bfloat16), grad_query)

    carry = entering(pieces, own, last, first, blocks[:, None] < blocks[None, :])
    grad_keys = mixed(back, quer, "bts,bta->bsa") + jnp.where(
        last_rows, mixed(value, carry, "bsc,bac->bsa"), 0.0
    )
    grad_values = mixed(attn, grad, "bts,btc->bsc") + jnp.where(
        last_rows, mixed(key, carry, "bsa,bac->bsc"), 0.0
    )
    rows = jnp.concatenate(
        [grad_query, grad_keys.astype(jnp.bfloat16), grad_values.astype(jnp.bfloat16)], -1
    )
    rows = rows.reshape(SUB * tok_rows, 3 * HS)
    packed = jnp.dot(
        place, rows, preferred_element_type=jnp.float32
    ).astype(jnp.bfloat16)
    halves = slots // 8
    packed = packed.reshape(seq_count, halves, 8, 3, HS).transpose(0, 1, 3, 2, 4)
    packed = packed.reshape(seq_count, halves * 12, 2, HS)
    packed = jnp.concatenate([packed, index], axis=1)
    received = lax.all_to_all(packed, "seq", 0, 0, tiled=True)
    index = received[::SUB, halves * 12, 0, :slots].astype(jnp.float32)
    choose = (index[None] == numbers[:, None, None]).astype(jnp.bfloat16)
    choose = choose.reshape(tok_rows, seq_count // SUB, halves, 8)
    received = received[:, : halves * 12].reshape(seq_count // SUB, SUB, halves, 3, 8, HS)
    return mixed(choose, received, "rghk,gshjkd->rjsd").astype(jnp.bfloat16).reshape(
        tok_rows, 3, width
    )


def solution(mesh):
    placed = (
        P("seq", "head"),
        P("seq", "head"),
        P("seq", "head"),
        P("seq", "head"),
        P("head"),
        P("seq"),
        P("seq"),
    )
    return jax.shard_map(
        local, mesh=mesh, in_specs=placed, out_specs=P("seq", None, "head"), check_vma=False
    )
```

```python
import jax
import jax.numpy as jnp
from jax import lax
from jax.experimental import pallas as pl
from jax.experimental.layout import Layout, with_layout_constraint
from jax.experimental.pallas import tpu as pltpu
from jax.sharding import PartitionSpec as P

HEADS = 32
HS = 128
EPSILON = 1e-05
SUB = 4
EXTRA = 8


def mixed(left, right, form):
    return jnp.einsum(form, left, right, preferred_element_type=jnp.float32)


def heads_first(array):
    return jnp.stack([array[:, at : at + HS] for at in range(0, array.shape[1], HS)])


def prepare(key_ref, value_ref, doc_ref, home_ref, out_ref):
    tok_rows = key_ref.shape[0]
    for s in range(SUB):
        out_ref[s, :tok_rows] = key_ref[:, s * HS : (s + 1) * HS]
        out_ref[s, tok_rows : 2 * tok_rows] = value_ref[:, s * HS : (s + 1) * HS]
    doc = doc_ref[...].astype(jnp.float32)
    home = home_ref[...]
    owner = lax.shift_right_logical(home, tok_rows.bit_length() - 1).astype(jnp.float32)
    target_row = (home & (tok_rows - 1)).astype(jnp.float32)
    across = jnp.broadcast_to(owner, (tok_rows, tok_rows))
    above = lax.broadcasted_iota(jnp.int32, across.shape, 0)
    along = lax.broadcasted_iota(jnp.int32, across.shape, 1)
    earlier = (across == across.T) & (above < along)
    ranks = jnp.sum(jnp.where(earlier, 1.0, 0.0), axis=0, keepdims=True)
    first = jnp.min(doc, axis=1, keepdims=True)
    last = jnp.max(doc, axis=1, keepdims=True)
    line = lax.broadcasted_iota(jnp.int32, (EXTRA, tok_rows), 0)
    small = jnp.zeros((EXTRA, tok_rows), jnp.float32)
    for at, value in enumerate((doc, owner, ranks, first, last, target_row)):
        small = jnp.where(line == at, value, small)
    for s in range(SUB):
        out_ref[s, 2 * tok_rows :] = small.astype(jnp.bfloat16)


def together(*values):
    return lax.optimization_barrier(values)


def local(query, keys, values, grad_normed, norm_gain, doc_ids, home):
    tok_rows, width = query.shape
    full_width = HEADS * HS
    seq_count = lax.axis_size("seq")
    head_count = lax.axis_size("head")
    capacity = 2 * tok_rows // seq_count
    slots = SUB * capacity
    groups = [[g * SUB + s for s in range(SUB)] for g in range(seq_count // SUB)]
    wide_groups = [[i * head_count + h for i in one for h in range(head_count)] for one in groups]
    places = jnp.arange(tok_rows)
    blocks = jnp.arange(SUB)

    def regroup(array):
        return lax.all_to_all(array, "seq", 0, 0, tiled=True, axis_index_groups=groups)

    key_value = pl.pallas_call(
        prepare,
        out_shape=jax.ShapeDtypeStruct((SUB, 2 * tok_rows + EXTRA, HS), jnp.bfloat16),
        in_specs=[pl.BlockSpec(memory_space=pltpu.VMEM)] * 4,
        out_specs=pl.BlockSpec(memory_space=pltpu.VMEM),
    )(keys, values, doc_ids.reshape(1, -1), home.reshape(1, -1))
    key_value = regroup(key_value)
    key = key_value[:, :tok_rows]
    value = key_value[:, tok_rows : 2 * tok_rows]
    small = key_value[:, 2 * tok_rows :].astype(jnp.float32)
    doc = small[:, 0]
    gain = norm_gain.reshape(SUB, HS)
    gain = jnp.sum(jnp.where((blocks == lax.axis_index("seq") % SUB)[:, None], gain, 0.0), axis=0)

    first, last = small[:, 3], small[:, 4]
    first_rows = (doc == first)[:, :, None]
    last_rows = (doc == last)[:, :, None]
    zero = jnp.zeros((), jnp.bfloat16)

    def shifted(load, groups_on):
        step = groups_on * SUB
        pairs = [(i, i + step) for i in range(seq_count) if 0 <= i + step < seq_count]
        return lax.ppermute(load, "seq", pairs)

    def payload(state, number):
        number = jnp.broadcast_to(number.astype(jnp.bfloat16), (EXTRA, HS))
        return jnp.concatenate([state.astype(jnp.bfloat16), number], axis=0)

    def entering(pieces, own, numbers, own_numbers, order):
        state = sum(
            jnp.where(
                p[HS : HS + 1].astype(jnp.float32)[None] == numbers[:, None],
                p[:HS].astype(jnp.float32)[None],
                0.0,
            )
            for p in pieces
        )
        joined = order[:, :, None] & (numbers[:, None] == own_numbers[None, :])
        inside = jnp.sum(jnp.where(joined[:, :, None], own[None], 0.0), axis=1)
        return (state + inside).astype(jnp.bfloat16)

    sent = mixed(jnp.where((doc == last[SUB - 1])[:, :, None], key, zero), value, "bta,btc->ac")
    near = shifted(payload(sent, last[SUB - 1]), 1)
    pieces = [near, shifted(near, 1)]
    own = mixed(jnp.where(last_rows, key, zero), value, "bta,btc->bac")
    query_grad = jnp.concatenate([heads_first(query), heads_first(grad_normed)], axis=1)
    numbers, lanes, all_slots, all_owners, starts = (
        count.astype(jnp.float32)
        for count in (
            places + 1,
            jnp.arange(HS),
            jnp.arange(seq_count * slots),
            jnp.arange(seq_count),
            blocks * capacity,
        )
    )
    query_grad, own, numbers, lanes, all_slots, all_owners, starts = together(
        query_grad, own, numbers, lanes, all_slots, all_owners, starts
    )
    query_grad = regroup(query_grad)
    quer = query_grad[:, :tok_rows]
    normed = query_grad[:, tok_rows:]
    visible = (doc[:, :, None] == doc[:, None, :]) & (places[:, None] >= places[None, :])
    attn = jnp.where(visible, mixed(quer, key, "bta,bsa->bts"), 0.0).astype(jnp.bfloat16)
    carry = entering(pieces, own, first, last, blocks[:, None] > blocks[None, :])
    output = mixed(attn, value, "bts,bsc->btc") + jnp.where(
        first_rows, mixed(quer, carry, "bta,bac->btc"), 0.0
    )
    scaled = gain * normed.astype(jnp.float32)
    sums = jnp.concatenate([jnp.sum(output * output, -1), jnp.sum(scaled * output, -1)])
    sums = jnp.broadcast_to(sums[None], (SUB * head_count, 2 * SUB, tok_rows))
    sums = lax.all_to_all(
        sums, ("seq", "head"), 0, 0, tiled=True, axis_index_groups=wide_groups
    ).sum(0)
    squares, inner = sums[:SUB, :, None], sums[SUB:, :, None]
    inv_rms = lax.rsqrt(squares / full_width + EPSILON)
    grad = (
        inv_rms * scaled - output * (inv_rms * inv_rms * inv_rms * inner / full_width)
    ).astype(jnp.bfloat16)

    sent = mixed(jnp.where((doc == first[0])[:, :, None], quer, zero), grad, "bta,btc->ac")
    sent = payload(sent, first[0])
    pieces = [shifted(sent, -1), shifted(sent, -2)]
    back = jnp.where(visible, mixed(grad, value, "btc,bsc->bts"), 0.0).astype(jnp.bfloat16)
    grad_query = mixed(back, key, "bts,bsa->bta") + jnp.where(
        first_rows, mixed(grad, carry, "btc,bac->bta"), 0.0
    )
    grad_query = grad_query.astype(jnp.bfloat16)
    own = mixed(jnp.where(first_rows, quer, zero), grad, "bta,btc->bac")

    small, grad = together(small, grad)
    owners, ranks, row = (small[:, at].reshape(-1) for at in (1, 2, 5))
    rank_slot = (small[:, 2] + starts[:, None]).reshape(-1)
    slot = owners * slots + rank_slot
    place = slot[None, :] == all_slots[:, None]
    to_owner = owners[None, :] == all_owners[:, None]
    at_slot = rank_slot[:, None] == lanes[None, :]
    index = jnp.dot(
        to_owner.astype(jnp.bfloat16),
        jnp.where(at_slot, row[:, None] + 1.0, 0.0).astype(jnp.bfloat16),
        preferred_element_type=jnp.float32,
    ).astype(jnp.bfloat16)
    tiles = slots // 8 * 12
    index = jnp.pad(index[:, None, None], ((0, 0), (tiles, 0), (0, 1), (0, 0)))
    index = with_layout_constraint(index, Layout((0, 1, 2, 3)))
    index, place, grad_query = together(index, place.astype(jnp.bfloat16), grad_query)

    carry = entering(pieces, own, last, first, blocks[:, None] < blocks[None, :])
    grad_keys = mixed(back, quer, "bts,bta->bsa") + jnp.where(
        last_rows, mixed(value, carry, "bsc,bac->bsa"), 0.0
    )
    grad_values = mixed(attn, grad, "bts,btc->bsc") + jnp.where(
        last_rows, mixed(key, carry, "bsa,bac->bsc"), 0.0
    )
    rows = jnp.concatenate(
        [grad_query, grad_keys.astype(jnp.bfloat16), grad_values.astype(jnp.bfloat16)], -1
    )
    rows = rows.reshape(SUB * tok_rows, 3 * HS)
    packed = jnp.dot(
        place, rows, preferred_element_type=jnp.float32
    ).astype(jnp.bfloat16)
    halves = slots // 8
    packed = packed.reshape(seq_count, halves, 8, 3, HS).transpose(0, 1, 3, 2, 4)
    packed = packed.reshape(seq_count, halves * 12, 2, HS)
    packed = lax.dynamic_update_slice(index, packed, (0, 0, 0, 0))
    received = lax.all_to_all(packed, "seq", 0, 0, tiled=True)
    index = received[::SUB, halves * 12, 0, :slots].astype(jnp.float32)
    choose = (index[None] == numbers[:, None, None]).astype(jnp.bfloat16)
    choose = choose.reshape(tok_rows, seq_count // SUB * slots)
    received = received[:, : halves * 12].reshape(seq_count // SUB, SUB, halves, 3, 8, HS)
    received = received.transpose(3, 0, 2, 4, 1, 5).reshape(3, seq_count // SUB * slots, width)
    rows = mixed(choose, received, "rk,jkn->jrn").astype(jnp.bfloat16)
    return rows.transpose(1, 0, 2)


def solution(mesh):
    placed = (
        P("seq", "head"),
        P("seq", "head"),
        P("seq", "head"),
        P("seq", "head"),
        P("head"),
        P("seq"),
        P("seq"),
    )
    return jax.shard_map(
        local, mesh=mesh, in_specs=placed, out_specs=P("seq", None, "head"), check_vma=False
    )
```

```python
import jax
import jax.numpy as jnp
from jax import lax
from jax.experimental import pallas as pl
from jax.experimental.layout import Layout, with_layout_constraint
from jax.experimental.pallas import tpu as pltpu
from jax.sharding import PartitionSpec as P

HEADS = 32
HS = 128
EPSILON = 1e-05
SUB = 4
EXTRA = 8


def mixed(left, right, form):
    return jnp.einsum(form, left, right, preferred_element_type=jnp.float32)


def heads_first(array):
    return jnp.stack([array[:, at : at + HS] for at in range(0, array.shape[1], HS)])


def prepare(key_ref, value_ref, doc_ref, home_ref, out_ref):
    tok_rows = key_ref.shape[0]
    for s in range(SUB):
        out_ref[s, :tok_rows] = key_ref[:, s * HS : (s + 1) * HS]
        out_ref[s, tok_rows : 2 * tok_rows] = value_ref[:, s * HS : (s + 1) * HS]
    doc = doc_ref[...].astype(jnp.float32)
    home = home_ref[...]
    owner = lax.shift_right_logical(home, tok_rows.bit_length() - 1).astype(jnp.float32)
    target_row = (home & (tok_rows - 1)).astype(jnp.float32)
    across = jnp.broadcast_to(owner, (tok_rows, tok_rows))
    above = lax.broadcasted_iota(jnp.int32, across.shape, 0)
    along = lax.broadcasted_iota(jnp.int32, across.shape, 1)
    earlier = (across == across.T) & (above < along)
    ranks = jnp.sum(jnp.where(earlier, 1.0, 0.0), axis=0, keepdims=True)
    first = jnp.min(doc, axis=1, keepdims=True)
    last = jnp.max(doc, axis=1, keepdims=True)
    line = lax.broadcasted_iota(jnp.int32, (EXTRA, tok_rows), 0)
    small = jnp.zeros((EXTRA, tok_rows), jnp.float32)
    for at, value in enumerate((doc, owner, ranks, first, last, target_row)):
        small = jnp.where(line == at, value, small)
    for s in range(SUB):
        out_ref[s, 2 * tok_rows :] = small.astype(jnp.bfloat16)


def together(*values):
    return lax.optimization_barrier(values)


def local(query, keys, values, grad_normed, norm_gain, doc_ids, home):
    tok_rows, width = query.shape
    full_width = HEADS * HS
    seq_count = lax.axis_size("seq")
    head_count = lax.axis_size("head")
    capacity = 2 * tok_rows // seq_count
    slots = SUB * capacity
    groups = [[g * SUB + s for s in range(SUB)] for g in range(seq_count // SUB)]
    wide_groups = [[i * head_count + h for i in one for h in range(head_count)] for one in groups]
    places = jnp.arange(tok_rows)
    blocks = jnp.arange(SUB)

    def regroup(array):
        return lax.all_to_all(array, "seq", 0, 0, tiled=True, axis_index_groups=groups)

    key_value = pl.pallas_call(
        prepare,
        out_shape=jax.ShapeDtypeStruct((SUB, 2 * tok_rows + EXTRA, HS), jnp.bfloat16),
        in_specs=[pl.BlockSpec(memory_space=pltpu.VMEM)] * 4,
        out_specs=pl.BlockSpec(memory_space=pltpu.VMEM),
    )(keys, values, doc_ids.reshape(1, -1), home.reshape(1, -1))
    key_value = regroup(key_value)
    key = key_value[:, :tok_rows]
    value = key_value[:, tok_rows : 2 * tok_rows]
    small = key_value[:, 2 * tok_rows :].astype(jnp.float32)
    doc = small[:, 0]
    gain = norm_gain.reshape(SUB, HS)
    gain = jnp.sum(jnp.where((blocks == lax.axis_index("seq") % SUB)[:, None], gain, 0.0), axis=0)

    first, last = small[:, 3], small[:, 4]
    first_rows = (doc == first)[:, :, None]
    last_rows = (doc == last)[:, :, None]
    zero = jnp.zeros((), jnp.bfloat16)

    def shifted(load, groups_on):
        step = groups_on * SUB
        pairs = [(i, i + step) for i in range(seq_count) if 0 <= i + step < seq_count]
        return lax.ppermute(load, "seq", pairs)

    def payload(state, number):
        number = jnp.broadcast_to(number.astype(jnp.bfloat16), (EXTRA, HS))
        return jnp.concatenate([state.astype(jnp.bfloat16), number], axis=0)

    def entering(pieces, own, numbers, own_numbers, order):
        state = sum(
            jnp.where(
                p[HS : HS + 1].astype(jnp.float32)[None] == numbers[:, None],
                p[:HS].astype(jnp.float32)[None],
                0.0,
            )
            for p in pieces
        )
        joined = order[:, :, None] & (numbers[:, None] == own_numbers[None, :])
        inside = jnp.sum(jnp.where(joined[:, :, None], own[None], 0.0), axis=1)
        return (state + inside).astype(jnp.bfloat16)

    sent = mixed(jnp.where((doc == last[SUB - 1])[:, :, None], key, zero), value, "bta,btc->ac")
    near = shifted(payload(sent, last[SUB - 1]), 1)
    pieces = [near, shifted(near, 1)]
    own = mixed(jnp.where(last_rows, key, zero), value, "bta,btc->bac")
    query_grad = jnp.concatenate([heads_first(query), heads_first(grad_normed)], axis=1)
    numbers, lanes, all_slots, all_owners, starts = (
        count.astype(jnp.float32)
        for count in (
            places + 1,
            jnp.arange(HS),
            jnp.arange(seq_count * slots),
            jnp.arange(seq_count),
            blocks * capacity,
        )
    )
    query_grad, own, numbers, lanes, all_slots, all_owners, starts = together(
        query_grad, own, numbers, lanes, all_slots, all_owners, starts
    )
    query_grad = regroup(query_grad)
    quer = query_grad[:, :tok_rows]
    normed = query_grad[:, tok_rows:]
    visible = (doc[:, :, None] == doc[:, None, :]) & (places[:, None] >= places[None, :])
    attn = jnp.where(visible, mixed(quer, key, "bta,bsa->bts"), 0.0).astype(jnp.bfloat16)
    carry = entering(pieces, own, first, last, blocks[:, None] > blocks[None, :])
    output = mixed(attn, value, "bts,bsc->btc") + jnp.where(
        first_rows, mixed(quer, carry, "bta,bac->btc"), 0.0
    )
    scaled = gain * normed.astype(jnp.float32)
    sums = jnp.concatenate([jnp.sum(output * output, -1), jnp.sum(scaled * output, -1)])
    sums = jnp.broadcast_to(sums[None], (SUB * head_count, 2 * SUB, tok_rows))
    sums = lax.all_to_all(
        sums, ("seq", "head"), 0, 0, tiled=True, axis_index_groups=wide_groups
    ).sum(0)
    squares, inner = sums[:SUB, :, None], sums[SUB:, :, None]
    inv_rms = lax.rsqrt(squares / full_width + EPSILON)
    grad = (
        inv_rms * scaled - output * (inv_rms * inv_rms * inv_rms * inner / full_width)
    ).astype(jnp.bfloat16)

    sent = mixed(jnp.where((doc == first[0])[:, :, None], quer, zero), grad, "bta,btc->ac")
    sent = payload(sent, first[0])
    pieces = [shifted(sent, -1), shifted(sent, -2)]
    back = jnp.where(visible, mixed(grad, value, "btc,bsc->bts"), 0.0).astype(jnp.bfloat16)
    grad_query = mixed(back, key, "bts,bsa->bta") + jnp.where(
        first_rows, mixed(grad, carry, "btc,bac->bta"), 0.0
    )
    grad_query = grad_query.astype(jnp.bfloat16)
    own = mixed(jnp.where(first_rows, quer, zero), grad, "bta,btc->bac")

    small, grad = together(small, grad)
    owners, ranks, row = (small[:, at].reshape(-1) for at in (1, 2, 5))
    rank_slot = (small[:, 2] + starts[:, None]).reshape(-1)
    slot = owners * slots + rank_slot
    place = slot[None, :] == all_slots[:, None]
    to_owner = owners[None, :] == all_owners[:, None]
    at_slot = rank_slot[:, None] == lanes[None, :]
    index = jnp.dot(
        to_owner.astype(jnp.bfloat16),
        jnp.where(at_slot, row[:, None] + 1.0, 0.0).astype(jnp.bfloat16),
        preferred_element_type=jnp.float32,
    ).astype(jnp.bfloat16)
    tiles = slots // 8 * 12
    index = jnp.pad(index[:, None, None], ((0, 0), (tiles, 0), (0, 1), (0, 0)))
    index = with_layout_constraint(index, Layout((0, 1, 2, 3)))
    index, place, grad_query = together(index, place.astype(jnp.bfloat16), grad_query)

    halves = slots // 8

    def put(buffer, rows, at):
        arrays = rows.shape[-1] // HS
        packed = jnp.dot(
            place, rows.reshape(SUB * tok_rows, arrays * HS), preferred_element_type=jnp.float32
        ).astype(jnp.bfloat16)
        packed = packed.reshape(seq_count, halves, 8, arrays, HS).transpose(0, 1, 3, 2, 4)
        packed = packed.reshape(seq_count, halves * arrays * 4, 2, HS)
        return lax.dynamic_update_slice(buffer, packed, (0, halves * at * 4, 0, 0))

    packed = put(index, grad_query, 0)

    carry = entering(pieces, own, last, first, blocks[:, None] < blocks[None, :])
    grad_keys = mixed(back, quer, "bts,bta->bsa") + jnp.where(
        last_rows, mixed(value, carry, "bsc,bac->bsa"), 0.0
    )
    grad_values = mixed(attn, grad, "bts,btc->bsc") + jnp.where(
        last_rows, mixed(key, carry, "bsa,bac->bsc"), 0.0
    )
    rows = jnp.concatenate([grad_keys.astype(jnp.bfloat16), grad_values.astype(jnp.bfloat16)], -1)
    packed = put(packed, rows, 1)
    received = lax.all_to_all(packed, "seq", 0, 0, tiled=True)
    index = received[::SUB, halves * 12, 0, :slots].astype(jnp.float32)
    choose = (index[None] == numbers[:, None, None]).astype(jnp.bfloat16)
    choose = choose.reshape(tok_rows, seq_count // SUB * slots)
    parts = []
    for at, arrays in ((0, 1), (1, 2)):
        part = received[:, halves * at * 4 : halves * (at + arrays) * 4]
        part = part.reshape(seq_count // SUB, SUB, halves, arrays, 8, HS).transpose(3, 0, 2, 4, 1, 5)
        parts.append(part.reshape(arrays, seq_count // SUB * slots, width))
    received = jnp.concatenate(parts)
    rows = mixed(choose, received, "rk,jkn->jrn").astype(jnp.bfloat16)
    return rows.transpose(1, 0, 2)


def solution(mesh):
    placed = (
        P("seq", "head"),
        P("seq", "head"),
        P("seq", "head"),
        P("seq", "head"),
        P("head"),
        P("seq"),
        P("seq"),
    )
    return jax.shard_map(
        local, mesh=mesh, in_specs=placed, out_specs=P("seq", None, "head"), check_vma=False
    )
```

```python
import jax
import jax.numpy as jnp
from jax import lax
from jax.experimental import pallas as pl
from jax.experimental.layout import Layout, with_layout_constraint
from jax.experimental.pallas import tpu as pltpu
from jax.sharding import PartitionSpec as P

HEADS = 32
HS = 128
EPSILON = 1e-05
SUB = 4
EXTRA = 8


def mixed(left, right, form):
    return jnp.einsum(form, left, right, preferred_element_type=jnp.float32)


def heads_first(array):
    return jnp.stack([array[:, at : at + HS] for at in range(0, array.shape[1], HS)])


def prepare(key_ref, value_ref, doc_ref, home_ref, out_ref):
    tok_rows = key_ref.shape[0]
    for s in range(SUB):
        out_ref[s, :tok_rows] = key_ref[:, s * HS : (s + 1) * HS]
        out_ref[s, tok_rows : 2 * tok_rows] = value_ref[:, s * HS : (s + 1) * HS]
    doc = doc_ref[...].astype(jnp.float32)
    home = home_ref[...]
    owner = lax.shift_right_logical(home, tok_rows.bit_length() - 1).astype(jnp.float32)
    target_row = (home & (tok_rows - 1)).astype(jnp.float32)
    across = jnp.broadcast_to(owner, (tok_rows, tok_rows))
    above = lax.broadcasted_iota(jnp.int32, across.shape, 0)
    along = lax.broadcasted_iota(jnp.int32, across.shape, 1)
    earlier = (across == across.T) & (above < along)
    ranks = jnp.sum(jnp.where(earlier, 1.0, 0.0), axis=0, keepdims=True)
    first = jnp.min(doc, axis=1, keepdims=True)
    last = jnp.max(doc, axis=1, keepdims=True)
    line = lax.broadcasted_iota(jnp.int32, (EXTRA, tok_rows), 0)
    small = jnp.zeros((EXTRA, tok_rows), jnp.float32)
    for at, value in enumerate((doc, owner, ranks, first, last, target_row)):
        small = jnp.where(line == at, value, small)
    for s in range(SUB):
        out_ref[s, 2 * tok_rows :] = small.astype(jnp.bfloat16)


def together(*values):
    return lax.optimization_barrier(values)


def local(query, keys, values, grad_normed, norm_gain, doc_ids, home):
    tok_rows, width = query.shape
    full_width = HEADS * HS
    seq_count = lax.axis_size("seq")
    head_count = lax.axis_size("head")
    capacity = 2 * tok_rows // seq_count
    slots = SUB * capacity
    groups = [[g * SUB + s for s in range(SUB)] for g in range(seq_count // SUB)]
    wide_groups = [[i * head_count + h for h in range(head_count) for i in one] for one in groups]
    places = jnp.arange(tok_rows)
    blocks = jnp.arange(SUB)

    def regroup(array):
        return lax.all_to_all(array, "seq", 0, 0, tiled=True, axis_index_groups=groups)

    key_value = pl.pallas_call(
        prepare,
        out_shape=jax.ShapeDtypeStruct((SUB, 2 * tok_rows + EXTRA, HS), jnp.bfloat16),
        in_specs=[pl.BlockSpec(memory_space=pltpu.VMEM)] * 4,
        out_specs=pl.BlockSpec(memory_space=pltpu.VMEM),
    )(keys, values, doc_ids.reshape(1, -1), home.reshape(1, -1))
    key_value = regroup(key_value)
    key = key_value[:, :tok_rows]
    value = key_value[:, tok_rows : 2 * tok_rows]
    small = key_value[:, 2 * tok_rows :].astype(jnp.float32)
    doc = small[:, 0]
    gain = norm_gain.reshape(SUB, HS)
    gain = jnp.sum(jnp.where((blocks == lax.axis_index("seq") % SUB)[:, None], gain, 0.0), axis=0)

    first, last = small[:, 3], small[:, 4]
    first_rows = (doc == first)[:, :, None]
    last_rows = (doc == last)[:, :, None]
    zero = jnp.zeros((), jnp.bfloat16)

    def shifted(load, groups_on):
        step = groups_on * SUB
        pairs = [(i, i + step) for i in range(seq_count) if 0 <= i + step < seq_count]
        return lax.ppermute(load, "seq", pairs)

    def payload(state, number):
        number = jnp.broadcast_to(number.astype(jnp.bfloat16), (EXTRA, HS))
        return jnp.concatenate([state.astype(jnp.bfloat16), number], axis=0)

    def entering(pieces, own, numbers, own_numbers, order):
        state = sum(
            jnp.where(
                p[HS : HS + 1].astype(jnp.float32)[None] == numbers[:, None],
                p[:HS].astype(jnp.float32)[None],
                0.0,
            )
            for p in pieces
        )
        joined = order[:, :, None] & (numbers[:, None] == own_numbers[None, :])
        inside = jnp.sum(jnp.where(joined[:, :, None], own[None], 0.0), axis=1)
        return (state + inside).astype(jnp.bfloat16)

    sent = mixed(jnp.where((doc == last[SUB - 1])[:, :, None], key, zero), value, "bta,btc->ac")
    near = shifted(payload(sent, last[SUB - 1]), 1)
    pieces = [near, shifted(near, 1)]
    own = mixed(jnp.where(last_rows, key, zero), value, "bta,btc->bac")
    query_grad = jnp.concatenate([heads_first(query), heads_first(grad_normed)], axis=1)
    numbers, lanes, all_slots, all_owners, starts = (
        count.astype(jnp.float32)
        for count in (
            places + 1,
            jnp.arange(HS),
            jnp.arange(seq_count * slots),
            jnp.arange(seq_count),
            blocks * capacity,
        )
    )
    query_grad, own, numbers, lanes, all_slots, all_owners, starts = together(
        query_grad, own, numbers, lanes, all_slots, all_owners, starts
    )
    query_grad = regroup(query_grad)
    quer = query_grad[:, :tok_rows]
    normed = query_grad[:, tok_rows:]
    visible = (doc[:, :, None] == doc[:, None, :]) & (places[:, None] >= places[None, :])
    attn = jnp.where(visible, mixed(quer, key, "bta,bsa->bts"), 0.0).astype(jnp.bfloat16)
    carry = entering(pieces, own, first, last, blocks[:, None] > blocks[None, :])
    output = mixed(attn, value, "bts,bsc->btc") + jnp.where(
        first_rows, mixed(quer, carry, "bta,bac->btc"), 0.0
    )
    scaled = gain * normed.astype(jnp.float32)
    sums = jnp.concatenate([jnp.sum(output * output, -1), jnp.sum(scaled * output, -1)])
    sums = jnp.broadcast_to(sums[None], (SUB * head_count, 2 * SUB, tok_rows))
    sums = lax.all_to_all(
        sums, ("seq", "head"), 0, 0, tiled=True, axis_index_groups=wide_groups
    ).sum(0)
    squares, inner = sums[:SUB, :, None], sums[SUB:, :, None]
    inv_rms = lax.rsqrt(squares / full_width + EPSILON)
    grad = (
        inv_rms * scaled - output * (inv_rms * inv_rms * inv_rms * inner / full_width)
    ).astype(jnp.bfloat16)

    sent = mixed(jnp.where((doc == first[0])[:, :, None], quer, zero), grad, "bta,btc->ac")
    sent = payload(sent, first[0])
    pieces = [shifted(sent, -1), shifted(sent, -2)]
    back = jnp.where(visible, mixed(grad, value, "btc,bsc->bts"), 0.0).astype(jnp.bfloat16)
    grad_query = mixed(back, key, "bts,bsa->bta") + jnp.where(
        first_rows, mixed(grad, carry, "btc,bac->bta"), 0.0
    )
    grad_query = grad_query.astype(jnp.bfloat16)
    own = mixed(jnp.where(first_rows, quer, zero), grad, "bta,btc->bac")

    small, grad = together(small, grad)
    owners, ranks, row = (small[:, at].reshape(-1) for at in (1, 2, 5))
    rank_slot = (small[:, 2] + starts[:, None]).reshape(-1)
    slot = owners * slots + rank_slot
    place = slot[None, :] == all_slots[:, None]
    to_owner = owners[None, :] == all_owners[:, None]
    at_slot = rank_slot[:, None] == lanes[None, :]
    index = jnp.dot(
        to_owner.astype(jnp.bfloat16),
        jnp.where(at_slot, row[:, None] + 1.0, 0.0).astype(jnp.bfloat16),
        preferred_element_type=jnp.float32,
    ).astype(jnp.bfloat16)
    tiles = slots // 8 * 12
    index = jnp.pad(index[:, None, None], ((0, 0), (tiles, 0), (0, 1), (0, 0)))
    index = with_layout_constraint(index, Layout((0, 1, 2, 3)))
    index, place, grad_query = together(index, place.astype(jnp.bfloat16), grad_query)

    halves = slots // 8

    def put(buffer, rows, at):
        arrays = rows.shape[-1] // HS
        packed = jnp.dot(
            place, rows.reshape(SUB * tok_rows, arrays * HS), preferred_element_type=jnp.float32
        ).astype(jnp.bfloat16)
        packed = packed.reshape(seq_count, halves, 8, arrays, HS).transpose(0, 1, 3, 2, 4)
        packed = packed.reshape(seq_count, halves * arrays * 4, 2, HS)
        return lax.dynamic_update_slice(buffer, packed, (0, halves * at * 4, 0, 0))

    packed = put(index, grad_query, 0)

    carry = entering(pieces, own, last, first, blocks[:, None] < blocks[None, :])
    grad_keys = mixed(back, quer, "bts,bta->bsa") + jnp.where(
        last_rows, mixed(value, carry, "bsc,bac->bsa"), 0.0
    )
    grad_values = mixed(attn, grad, "bts,btc->bsc") + jnp.where(
        last_rows, mixed(key, carry, "bsa,bac->bsc"), 0.0
    )
    rows = jnp.concatenate([grad_keys.astype(jnp.bfloat16), grad_values.astype(jnp.bfloat16)], -1)
    packed = put(packed, rows, 1)
    received = lax.all_to_all(packed, "seq", 0, 0, tiled=True)
    index = received[::SUB, halves * 12, 0, :slots].astype(jnp.float32)
    choose = (index[None] == numbers[:, None, None]).astype(jnp.bfloat16)
    choose = choose.reshape(tok_rows, seq_count // SUB * slots)
    parts = []
    for at, arrays in ((0, 1), (1, 2)):
        part = received[:, halves * at * 4 : halves * (at + arrays) * 4]
        part = part.reshape(seq_count // SUB, SUB, halves, arrays, 8, HS).transpose(3, 0, 2, 4, 1, 5)
        parts.append(part.reshape(arrays, seq_count // SUB * slots, width))
    received = jnp.concatenate(parts)
    rows = mixed(choose, received, "rk,jkn->jrn").astype(jnp.bfloat16)
    return rows.transpose(1, 0, 2)


def solution(mesh):
    placed = (
        P("seq", "head"),
        P("seq", "head"),
        P("seq", "head"),
        P("seq", "head"),
        P("head"),
        P("seq"),
        P("seq"),
    )
    return jax.shard_map(
        local, mesh=mesh, in_specs=placed, out_specs=P("seq", None, "head"), check_vma=False
    )
```

```python
import jax
import jax.numpy as jnp
from jax import lax
from jax.experimental import pallas as pl
from jax.experimental.layout import Layout, with_layout_constraint
from jax.experimental.pallas import tpu as pltpu
from jax.sharding import PartitionSpec as P

HEADS = 32
HS = 128
EPSILON = 1e-05
SUB = 4
EXTRA = 8


def mixed(left, right, form):
    return jnp.einsum(form, left, right, preferred_element_type=jnp.float32)


def heads_first(array):
    return jnp.stack([array[:, at : at + HS] for at in range(0, array.shape[1], HS)])


def prepare(key_ref, value_ref, doc_ref, home_ref, out_ref):
    tok_rows = key_ref.shape[0]
    for s in range(SUB):
        out_ref[s, :tok_rows] = key_ref[:, s * HS : (s + 1) * HS]
        out_ref[s, tok_rows : 2 * tok_rows] = value_ref[:, s * HS : (s + 1) * HS]
    doc = doc_ref[...].astype(jnp.float32)
    home = home_ref[...]
    owner = lax.shift_right_logical(home, tok_rows.bit_length() - 1).astype(jnp.float32)
    target_row = (home & (tok_rows - 1)).astype(jnp.float32)
    across = jnp.broadcast_to(owner, (tok_rows, tok_rows))
    above = lax.broadcasted_iota(jnp.int32, across.shape, 0)
    along = lax.broadcasted_iota(jnp.int32, across.shape, 1)
    earlier = (across == across.T) & (above < along)
    ranks = jnp.sum(jnp.where(earlier, 1.0, 0.0), axis=0, keepdims=True)
    first = jnp.min(doc, axis=1, keepdims=True)
    last = jnp.max(doc, axis=1, keepdims=True)
    line = lax.broadcasted_iota(jnp.int32, (EXTRA, tok_rows), 0)
    small = jnp.zeros((EXTRA, tok_rows), jnp.float32)
    for at, value in enumerate((doc, owner, ranks, first, last, target_row)):
        small = jnp.where(line == at, value, small)
    for s in range(SUB):
        out_ref[s, 2 * tok_rows :] = small.astype(jnp.bfloat16)


def together(*values):
    return lax.optimization_barrier(values)


def local(query, keys, values, grad_normed, norm_gain, doc_ids, home):
    tok_rows, width = query.shape
    full_width = HEADS * HS
    seq_count = lax.axis_size("seq")
    head_count = lax.axis_size("head")
    capacity = 2 * tok_rows // seq_count
    slots = SUB * capacity
    groups = [[g * SUB + s for s in range(SUB)] for g in range(seq_count // SUB)]
    wide_groups = [[i * head_count + h for h in reversed(range(head_count)) for i in one] for one in groups]
    places = jnp.arange(tok_rows)
    blocks = jnp.arange(SUB)

    def regroup(array):
        return lax.all_to_all(array, "seq", 0, 0, tiled=True, axis_index_groups=groups)

    key_value = pl.pallas_call(
        prepare,
        out_shape=jax.ShapeDtypeStruct((SUB, 2 * tok_rows + EXTRA, HS), jnp.bfloat16),
        in_specs=[pl.BlockSpec(memory_space=pltpu.VMEM)] * 4,
        out_specs=pl.BlockSpec(memory_space=pltpu.VMEM),
    )(keys, values, doc_ids.reshape(1, -1), home.reshape(1, -1))
    key_value = regroup(key_value)
    key = key_value[:, :tok_rows]
    value = key_value[:, tok_rows : 2 * tok_rows]
    small = key_value[:, 2 * tok_rows :].astype(jnp.float32)
    doc = small[:, 0]
    gain = norm_gain.reshape(SUB, HS)
    gain = jnp.sum(jnp.where((blocks == lax.axis_index("seq") % SUB)[:, None], gain, 0.0), axis=0)

    first, last = small[:, 3], small[:, 4]
    first_rows = (doc == first)[:, :, None]
    last_rows = (doc == last)[:, :, None]
    zero = jnp.zeros((), jnp.bfloat16)

    def shifted(load, groups_on):
        step = groups_on * SUB
        pairs = [(i, i + step) for i in range(seq_count) if 0 <= i + step < seq_count]
        return lax.ppermute(load, "seq", pairs)

    def payload(state, number):
        number = jnp.broadcast_to(number.astype(jnp.bfloat16), (EXTRA, HS))
        return jnp.concatenate([state.astype(jnp.bfloat16), number], axis=0)

    def entering(pieces, own, numbers, own_numbers, order):
        state = sum(
            jnp.where(
                p[HS : HS + 1].astype(jnp.float32)[None] == numbers[:, None],
                p[:HS].astype(jnp.float32)[None],
                0.0,
            )
            for p in pieces
        )
        joined = order[:, :, None] & (numbers[:, None] == own_numbers[None, :])
        inside = jnp.sum(jnp.where(joined[:, :, None], own[None], 0.0), axis=1)
        return (state + inside).astype(jnp.bfloat16)

    sent = mixed(jnp.where((doc == last[SUB - 1])[:, :, None], key, zero), value, "bta,btc->ac")
    near = shifted(payload(sent, last[SUB - 1]), 1)
    pieces = [near, shifted(near, 1)]
    own = mixed(jnp.where(last_rows, key, zero), value, "bta,btc->bac")
    query_grad = jnp.concatenate([heads_first(query), heads_first(grad_normed)], axis=1)
    numbers, lanes, all_slots, all_owners, starts = (
        count.astype(jnp.float32)
        for count in (
            places + 1,
            jnp.arange(HS),
            jnp.arange(seq_count * slots),
            jnp.arange(seq_count),
            blocks * capacity,
        )
    )
    query_grad, own, numbers, lanes, all_slots, all_owners, starts = together(
        query_grad, own, numbers, lanes, all_slots, all_owners, starts
    )
    query_grad = regroup(query_grad)
    quer = query_grad[:, :tok_rows]
    normed = query_grad[:, tok_rows:]
    visible = (doc[:, :, None] == doc[:, None, :]) & (places[:, None] >= places[None, :])
    attn = jnp.where(visible, mixed(quer, key, "bta,bsa->bts"), 0.0).astype(jnp.bfloat16)
    carry = entering(pieces, own, first, last, blocks[:, None] > blocks[None, :])
    output = mixed(attn, value, "bts,bsc->btc") + jnp.where(
        first_rows, mixed(quer, carry, "bta,bac->btc"), 0.0
    )
    scaled = gain * normed.astype(jnp.float32)
    sums = jnp.concatenate([jnp.sum(output * output, -1), jnp.sum(scaled * output, -1)])
    sums = jnp.broadcast_to(sums[None], (SUB * head_count, 2 * SUB, tok_rows))
    sums = lax.all_to_all(
        sums, ("seq", "head"), 0, 0, tiled=True, axis_index_groups=wide_groups
    ).sum(0)
    squares, inner = sums[:SUB, :, None], sums[SUB:, :, None]
    inv_rms = lax.rsqrt(squares / full_width + EPSILON)
    grad = (
        inv_rms * scaled - output * (inv_rms * inv_rms * inv_rms * inner / full_width)
    ).astype(jnp.bfloat16)

    sent = mixed(jnp.where((doc == first[0])[:, :, None], quer, zero), grad, "bta,btc->ac")
    sent = payload(sent, first[0])
    pieces = [shifted(sent, -1), shifted(sent, -2)]
    back = jnp.where(visible, mixed(grad, value, "btc,bsc->bts"), 0.0).astype(jnp.bfloat16)
    grad_query = mixed(back, key, "bts,bsa->bta") + jnp.where(
        first_rows, mixed(grad, carry, "btc,bac->bta"), 0.0
    )
    grad_query = grad_query.astype(jnp.bfloat16)
    own = mixed(jnp.where(first_rows, quer, zero), grad, "bta,btc->bac")

    small, grad = together(small, grad)
    owners, ranks, row = (small[:, at].reshape(-1) for at in (1, 2, 5))
    rank_slot = (small[:, 2] + starts[:, None]).reshape(-1)
    slot = owners * slots + rank_slot
    place = slot[None, :] == all_slots[:, None]
    to_owner = owners[None, :] == all_owners[:, None]
    at_slot = rank_slot[:, None] == lanes[None, :]
    index = jnp.dot(
        to_owner.astype(jnp.bfloat16),
        jnp.where(at_slot, row[:, None] + 1.0, 0.0).astype(jnp.bfloat16),
        preferred_element_type=jnp.float32,
    ).astype(jnp.bfloat16)
    tiles = slots // 8 * 12
    index = jnp.pad(index[:, None, None], ((0, 0), (tiles, 0), (0, 1), (0, 0)))
    index = with_layout_constraint(index, Layout((0, 1, 2, 3)))
    index, place, grad_query = together(index, place.astype(jnp.bfloat16), grad_query)

    halves = slots // 8

    def put(buffer, rows, at):
        arrays = rows.shape[-1] // HS
        packed = jnp.dot(
            place, rows.reshape(SUB * tok_rows, arrays * HS), preferred_element_type=jnp.float32
        ).astype(jnp.bfloat16)
        packed = packed.reshape(seq_count, halves, 8, arrays, HS).transpose(0, 1, 3, 2, 4)
        packed = packed.reshape(seq_count, halves * arrays * 4, 2, HS)
        return lax.dynamic_update_slice(buffer, packed, (0, halves * at * 4, 0, 0))

    packed = put(index, grad_query, 0)

    carry = entering(pieces, own, last, first, blocks[:, None] < blocks[None, :])
    grad_keys = mixed(back, quer, "bts,bta->bsa") + jnp.where(
        last_rows, mixed(value, carry, "bsc,bac->bsa"), 0.0
    )
    grad_values = mixed(attn, grad, "bts,btc->bsc") + jnp.where(
        last_rows, mixed(key, carry, "bsa,bac->bsc"), 0.0
    )
    rows = jnp.concatenate([grad_keys.astype(jnp.bfloat16), grad_values.astype(jnp.bfloat16)], -1)
    packed = put(packed, rows, 1)
    received = lax.all_to_all(packed, "seq", 0, 0, tiled=True)
    index = received[::SUB, halves * 12, 0, :slots].astype(jnp.float32)
    choose = (index[None] == numbers[:, None, None]).astype(jnp.bfloat16)
    choose = choose.reshape(tok_rows, seq_count // SUB * slots)
    parts = []
    for at, arrays in ((0, 1), (1, 2)):
        part = received[:, halves * at * 4 : halves * (at + arrays) * 4]
        part = part.reshape(seq_count // SUB, SUB, halves, arrays, 8, HS).transpose(3, 0, 2, 4, 1, 5)
        parts.append(part.reshape(arrays, seq_count // SUB * slots, width))
    received = jnp.concatenate(parts)
    rows = mixed(choose, received, "rk,jkn->jrn").astype(jnp.bfloat16)
    return rows.transpose(1, 0, 2)


def solution(mesh):
    placed = (
        P("seq", "head"),
        P("seq", "head"),
        P("seq", "head"),
        P("seq", "head"),
        P("head"),
        P("seq"),
        P("seq"),
    )
    return jax.shard_map(
        local, mesh=mesh, in_specs=placed, out_specs=P("seq", None, "head"), check_vma=False
    )
```
